768 devices in a mesh: mem: 64 (over z_hi, y, core), gx: 4 (over x), gy: 3 (over z_lo).
Axes of the slice: x: 4, y: 8, z: 12 (z_hi: 4, z_lo: 3; z = z_hi * 3 + z_lo), core: 2. Of those that a mesh axis runs over, the one named last changes fastest.
Arguments:
- gradient: float32 [192, 64, 384], P('mem', 'gx', 'gy'), may hold values from -6 to 6
- perturbation: bfloat16 [64, 192, 64, 384], P('mem', None, 'gx', 'gy'), may hold values from -16 to 16
- classes: int32 [2, 64, 384], P(None, 'gx', 'gy'), may hold values from 0 to 3
- land_sea: int32 [64, 384], P('gx', 'gy'), may hold values 0 or 1
Outputs:
- increment: float32 [192, 64, 384], P('mem', 'gx', 'gy')
The draws below stay inside these ranges and needn't reach their ends.
All inputs are finite; a program needn't handle non-finite values. No bound on the sum of `land_sea` on one device may be relied on, other than what follows from the above.
Results may differ from the reference program's by a relative error of at most 0.0005.
Values sent between devices are 32-bit elements; how exact they have to be, the bound alone decides.
A program may use at most 32 MiB of HBM per device.

```python
import jax
import jax.numpy as jnp
from jax import lax

SLOTS = 2
VARS = 3
LEVELS = 32
STEPS = 8
MEMBERS = 64
PLANES = 192
NX = 64
NY = 384


def touch_ends(result, key, low, high):
    longest = result.shape.index(max(result.shape))
    spots = []
    for shift in (0, 1):
        where = [jax.random.randint(jax.random.fold_in(key, axis), (), 0, length) for axis, length in enumerate(result.shape)]
        where[longest] = (where[longest] + shift) % result.shape[longest]
        spots.append(tuple(where))
    return result.at[spots[0]].set(low).at[spots[1]].set(high)


def raised(result, rng, source, target, parts, factor):
    owner, partner = [(jnp.arange(result.shape[axis_at]) // (result.shape[axis_at] // parts)).reshape([-1 if axis == axis_at else 1 for axis in range(result.ndim)]) for axis_at in (source, target)]
    chosen = jax.random.permutation(rng, parts)[partner]
    strong = (owner == chosen) | (owner == (partner + parts // 2) % parts)
    return jnp.where(strong, factor * result, result)


def block_levels(rng, shape, cuts, least, top_value):
    gain = 1.0
    for dim, shards_of in cuts:
        draws = jax.random.uniform(jax.random.fold_in(jax.random.fold_in(rng, 6), dim), (shards_of,), jnp.float32, least / len(cuts), top_value / len(cuts))
        gain = gain * jnp.repeat(jnp.exp(draws), shape[dim] // shards_of).reshape((-1,) + (1,) * (len(shape) - 1 - dim))
    return gain


def bell_draw(stream_key, shape, scale, reach, shards=(), kind=jnp.bfloat16):
    gain = block_levels(stream_key, shape, shards, -0.22, 0.18) if shards else 1.0
    drawn = jax.random.normal(stream_key, shape, jnp.float32) * scale * gain
    return jnp.minimum(jnp.maximum(drawn, -reach), reach).astype(kind)


def gaussian_with(key, dims, scale, limit, split, heavy, held_as=jnp.bfloat16):
    values = scale * jax.random.normal(key, dims, jnp.float32)
    if split:
        values = values * block_levels(key, dims, split, -0.22, 0.18)
    return jnp.clip(raised(values, jax.random.fold_in(key, 3), *heavy), -limit, limit).astype(held_as)


def setup_inputs(seed: int = 0) -> dict:
    key_list = jax.random.split(jax.random.key(seed), 5)
    return {
        "gradient": bell_draw(key_list[0], (PLANES, NX, NY), 1.0, 6.0, ((0, 64), (1, 4), (2, 3)), jnp.float32),
        "perturbation": gaussian_with(key_list[1], (MEMBERS, PLANES, NX, NY), 1.0, 16.0, ((0, 64), (2, 4), (3, 3)), (0, 1, 64, 4.0)),
        "classes": touch_ends(jax.random.randint(key_list[2], (2, NX, NY), 0, 4), jax.random.fold_in(key_list[2], 1), 0, 3).astype(jnp.int32),
        "land_sea": touch_ends((jax.random.randint(key_list[3], (NX, NY), 0, 10) < 7).astype(jnp.int32), jax.random.fold_in(key_list[3], 1), 0, 1),
    }


TABLE = (0.03, 0.07, 0.12, 0.18)


def lookup(code_map):
    return sum(TABLE[c] * (code_map == c + 1).astype(jnp.float32) for c in range(4))


def spread(field, coef_x, coef_y, inside):
    centre = field[:, 1:-1, 1:-1]
    centre_in = inside[1:-1, 1:-1]
    east_face = 0.5 * (coef_x[1:-1, 1:-1] + coef_x[2:, 1:-1]) * centre_in * inside[2:, 1:-1]
    west_face = 0.5 * (coef_x[1:-1, 1:-1] + coef_x[:-2, 1:-1]) * centre_in * inside[:-2, 1:-1]
    north_face = 0.5 * (coef_y[1:-1, 1:-1] + coef_y[1:-1, 2:]) * centre_in * inside[1:-1, 2:]
    south_face = 0.5 * (coef_y[1:-1, 1:-1] + coef_y[1:-1, :-2]) * centre_in * inside[1:-1, :-2]
    return (centre + east_face * (field[:, 2:, 1:-1] - centre) + west_face * (field[:, :-2, 1:-1] - centre)
            + north_face * (field[:, 1:-1, 2:] - centre) + south_face * (field[:, 1:-1, :-2] - centre))


def pad_field(field):
    return jnp.pad(field, ((0, 0), (1, 1), (1, 1)))


def reference(gradient, perturbation, classes, land_sea):
    members = perturbation.shape[0]
    code_map = jnp.stack([classes[0] + 1, classes[1] + 1, land_sea + 1]).astype(jnp.int32)
    padded = jnp.pad(code_map, ((0, 0), (1, 1), (1, 1)))
    coef_x = lookup(padded[0])
    coef_y = lookup(padded[1])
    inside = (padded[2] > 0).astype(jnp.float32)
    factor = jnp.where(land_sea == 1, jnp.float32(1.0), jnp.float32(0.3))
    groups = SLOTS * VARS

    def one_member(total, member_block):
        values = member_block.astype(jnp.float32)
        field = jnp.sum((values * gradient).reshape(groups, LEVELS, NX, NY), axis=0)
        for _ in range(STEPS):
            field = spread(pad_field(factor * field), coef_x, coef_y, inside)
        for _ in range(STEPS):
            field = factor * spread(pad_field(field), coef_x, coef_y, inside)
        return total + values * jnp.tile(field, (groups, 1, 1)) / jnp.float32(members - 1), None

    total, _ = lax.scan(one_member, jnp.zeros((PLANES, NX, NY), jnp.float32), perturbation)
    return total
```

```python
import functools

import jax
import jax.numpy as jnp
from jax import lax
from jax.experimental import pallas as pl
from jax.experimental.pallas import tpu as pltpu
from jax.sharding import PartitionSpec as P

LEVELS = 32
STEPS = 8
TABLE = (0.03, 0.07, 0.12, 0.18)
MESH = pl.DeviceIdType.MESH

ZH = 4
YN = 8
BLOCKS = ZH * YN
LONG = YN // 2
SHORT = YN - 1 - LONG
F32 = jnp.float32


def ag_lengths(dz):
    return (LONG, SHORT) if dz % 2 == 0 else (SHORT, LONG)


def rs_lengths(dz):
    return (LONG, SHORT) if dz % 2 == 1 else (SHORT, LONG)


def kernel(
    gx_n, gy_n, offsets,
    grad_hbm, pert_hbm, classes_hbm, sea_hbm, out_ref,
    gall, pown, praw, psend, pother, codes, coef,
    wsend, wrecv, wown, field, back, back_other, s_own, s_other,
    rs_send, rs_recv, rz_send, rz_recv,
    loc, agz_s, agz_r, agy_s, agy_r, code_s, code_r, px_s, px_r, w_s, w_r,
    t_s, t_r, b_s, b_r, fw_s, fw_r, rsy_s, rsy_r, rsz_s, rsz_r,
):
    mem = lax.axis_index("mem")
    gx = lax.axis_index("gx")
    gy = lax.axis_index("gy")
    core = lax.rem(mem, 2)
    y = lax.rem(mem // 2, YN)
    zh = mem // (2 * YN)
    zdir = 1 - 2 * core

    def mem_at(z, yy):
        return {"mem": (lax.rem(z + 2 * ZH, ZH) * YN + lax.rem(yy + 2 * YN, YN)) * 2 + core}

    partner = {"mem": mem + zdir}
    y_up, y_down = mem_at(zh, y + 1), mem_at(zh, y - 1)
    z_fwd, z_bwd = mem_at(zh + zdir, y), mem_at(zh - zdir, y)
    y_next = (y_up, y_down)

    def z_of(dz):
        return (zh, zh - zdir, zh + zdir, zh + 2)[dz]

    def block(z, yy):
        return lax.rem(z + 2 * ZH, ZH) * YN + lax.rem(yy + 2 * YN, YN)

    def tile_of(dx, dy):
        return lax.rem(gx + dx + gx_n, gx_n), lax.rem(gy + dy + gy_n, gy_n)

    def remote(src, dst, ssem, rsem, where):
        return pltpu.make_async_remote_copy(
            src_ref=src, dst_ref=dst, send_sem=ssem, recv_sem=rsem,
            device_id=where, device_id_type=MESH,
        )

    def window(ref, tx, ty):
        return ref.at[
            :, pl.ds(pl.multiple_of(tx * 16, 16), 16), pl.ds(pl.multiple_of(ty * 128, 128), 128)
        ]

    barrier = pltpu.get_barrier_semaphore()
    tiles = [tile_of(dx, dy) for dx, dy in offsets]
    for where in (z_fwd, z_bwd, y_up, y_down, partner):
        pl.semaphore_signal(barrier, inc=1, device_id=where, device_id_type=MESH)
    for tx, ty in tiles:
        pl.semaphore_signal(barrier, inc=1, device_id={"gx": tx, "gy": ty}, device_id_type=MESH)
    mine = block(zh, y)
    c_grad = pltpu.make_async_copy(grad_hbm, gall.at[mine], loc.at[0])
    c_cls = pltpu.make_async_copy(classes_hbm, window(codes, gx, gy).at[pl.ds(0, 2)], loc.at[1])
    c_sea = pltpu.make_async_copy(sea_hbm, window(codes, gx, gy).at[pl.ds(2, 1)], loc.at[2])
    c_raw = pltpu.make_async_copy(pert_hbm.at[:, 1 - core], praw, loc.at[3])
    c_own = pltpu.make_async_copy(pert_hbm.at[:, core], pown, loc.at[4])
    for copy in (c_grad, c_cls, c_sea, c_raw, c_own):
        copy.start()
    c_grad.wait()
    pl.semaphore_wait(barrier, 5 + len(offsets))

    def ag_z(k):
        source = (z_of(0), z_of(0), z_of(1))[k]
        at = gall.at[block(source, y)]
        return remote(at, at, agz_s.at[k], agz_r.at[k], (z_fwd, z_bwd, z_fwd)[k])

    def ag_z_in(k):
        at = gall.at[block(z_of((1, 2, 3)[k]), y)]
        return remote(at, at, agz_s.at[k], agz_r.at[k], z_fwd)

    def ag_y(dz, way, hop):
        source = y - hop if way == 0 else y + hop
        at = gall.at[block(z_of(dz), source)]
        return remote(at, at, agy_s.at[dz, way, hop], agy_r.at[dz, way, hop], y_next[way])

    def ag_y_in(dz, way, hop):
        source = y - hop - 1 if way == 0 else y + hop + 1
        at = gall.at[block(z_of(dz), source)]
        return remote(at, at, agy_s.at[dz, way, hop], agy_r.at[dz, way, hop], y_next[way])

    ag_z(0).start()
    ag_z(1).start()
    ag_y(0, 0, 0).start()
    ag_y(0, 1, 0).start()

    c_cls.wait()
    c_sea.wait()
    for i, (tx, ty) in enumerate(tiles):
        at = window(codes, gx, gy)
        remote(at, at, code_s.at[i], code_r.at[i], {"gx": tx, "gy": ty}).start()
    c_raw.wait()

    @pl.loop(0, BLOCKS)
    def _(b):
        psend[b] = praw[b].astype(F32)

    remote(psend, pother, px_s, px_r, partner).start()
    c_own.wait()

    z_time = {0: 0.0, 1: 3.5, 2: 3.5, 3: 7.0}
    events = [(z_time[dz], 0, dz, 0, 0) for dz in (1, 2, 3)]
    for dz in range(ZH):
        for way in (0, 1):
            for hop in range(ag_lengths(dz)[way]):
                events.append((z_time[dz] + 2.0 * (hop + 1), 1, dz, way, hop))
    events.sort()
    late = len(events) - 6
    for number, (_, kind, dz, way, hop) in enumerate(events):
        if number == late:
            coefficients(gx_n, gy_n, offsets, tile_of, window, remote, codes, coef, code_s, code_r)
        if kind == 0:
            ag_z_in(dz - 1).wait_recv()
            if dz == 1:
                ag_z(2).start()
            ag_y(dz, 0, 0).start()
            ag_y(dz, 1, 0).start()
        else:
            ag_y_in(dz, way, hop).wait_recv()
            if hop + 1 < ag_lengths(dz)[way]:
                ag_y(dz, way, hop + 1).start()

    def weights(p_ref, w_ref):
        @pl.loop(0, 16, unroll=4)
        def _(e):
            one = lax.rem(11 * e, 16)
            two = lax.rem(11 * (e + 15), 16)

            def part(b, i):
                return p_ref[b, i].astype(F32) * gall[b, i]

            w_ref[lax.rem(2 * e + 3 * core, LEVELS)] = (
                part(one, 0) + part(one + 16, 0) + part(two, 2) + part(two + 16, 2)
            )
            w_ref[lax.rem(2 * e + 1 + 3 * core, LEVELS)] = part(one, 1) + part(one + 16, 1)

    swap_p = remote(psend, pother, px_s, px_r, partner)
    swap_p.wait_recv()
    weights(pother, wsend)
    swap_w = remote(wsend, wrecv, w_s, w_r, partner)
    swap_w.start()
    weights(pown, wown)
    swap_w.wait_recv()
    wown[...] = wown[...] + wrecv[...]

    def first_level(tx, ty):
        return 8 * tx + jnp.minimum(3 * ty, 5)

    for i, (tx, ty) in enumerate(tiles):
        remote(
            wown.at[pl.ds(first_level(tx, ty), 3)], window(field.at[0], gx, gy),
            t_s.at[i], t_r.at[i], {"gx": tx, "gy": ty},
        ).start()
    c_field = pltpu.make_async_copy(
        wown.at[pl.ds(first_level(gx, gy), 3)], window(field.at[0], gx, gy), loc.at[0]
    )
    c_field.start()
    c_field.wait()
    for i, (dx, dy) in enumerate(offsets):
        sx, sy = tile_of(-dx, -dy)
        remote(
            wown.at[pl.ds(first_level(gx, gy), 3)], window(field.at[0], sx, sy),
            t_s.at[i], t_r.at[i], {"gx": sx, "gy": sy},
        ).wait_recv()

    def stencil(source, target, base):
        for lev in range(3):
            v = field[source, lev]
            rows, cols = v.shape
            field[target, lev] = (
                coef[0] * v
                + coef[base] * pltpu.roll(v, rows - 1, 0)
                + coef[base + 1] * pltpu.roll(v, 1, 0)
                + coef[base + 2] * pltpu.roll(v, cols - 1, 1)
                + coef[base + 3] * pltpu.roll(v, 1, 1)
            )

    for base in (1, 5):
        @pl.loop(0, STEPS // 2)
        def _(_):
            stencil(0, 1, base)
            stencil(1, 0, base)

    def back_at(ref, tx, ty):
        return ref.at[tx, pl.ds(3 * ty, 3)]

    for i, (tx, ty) in enumerate(tiles):
        remote(
            window(field.at[0], tx, ty), back_at(back, gx, gy), b_s.at[i], b_r.at[i],
            {"gx": tx, "gy": ty},
        ).start()
    c_back = pltpu.make_async_copy(window(field.at[0], gx, gy), back_at(back, gx, gy), loc.at[0])
    c_back.start()
    c_back.wait()

    def forward(i, tx, ty):
        return remote(
            back_at(back, tx, ty), back_at(back_other, tx, ty), fw_s.at[i], fw_r.at[i], partner
        )

    forward(len(offsets), gx, gy).start()
    for i, (dx, dy) in enumerate(offsets):
        sx, sy = tile_of(-dx, -dy)
        remote(
            window(field.at[0], sx, sy), back_at(back, sx, sy), b_s.at[i], b_r.at[i],
            {"gx": sx, "gy": sy},
        ).wait_recv()
        forward(i, sx, sy).start()

    def gathered(ref, s_ref):
        levels = jnp.concatenate([ref[:, 0:6], ref[:, 7:9]], axis=1) * F32(1.0 / 63.0)
        levels = levels.reshape((LEVELS,) + levels.shape[2:])
        s_ref[pl.ds(0, LEVELS)] = levels
        s_ref[pl.ds(LEVELS, 2)] = levels[0:2]

    gathered(back, s_own)
    for i, (dx, dy) in enumerate(offsets):
        sx, sy = tile_of(-dx, -dy)
        forward(i, sx, sy).wait_recv()
    forward(len(offsets), gx, gy).wait_recv()
    gathered(back_other, s_other)

    def term(dz, yy):
        b = block(z_of(dz), yy)
        levels = pl.ds(lax.rem(6 * b + 3 * core, LEVELS), 3)
        return pown[b].astype(F32) * s_own[levels] + pother[b] * s_other[levels]

    def rs_y(dz, way, hop):
        return remote(
            rs_send.at[dz, way, hop], rs_recv.at[dz, way, hop],
            rsy_s.at[dz, way, hop], rsy_r.at[dz, way, hop], y_next[way],
        )

    def rs_z(k):
        return remote(
            rz_send.at[k], rz_recv.at[k], rsz_s.at[k], rsz_r.at[k], (z_fwd, z_fwd, z_bwd)[k]
        )

    order = (3, 2, 1, 0)
    for hop in range(LONG + 1):
        for dz in order:
            for way in (0, 1):
                left = rs_lengths(dz)[way] - hop
                if left > 0:
                    value = term(dz, y + left if way == 0 else y - left)
                    if hop > 0:
                        rs_y(dz, way, hop - 1).wait_recv()
                        value = value + rs_recv[dz, way, hop - 1]
                    rs_send[dz, way, hop] = value
                    rs_y(dz, way, hop).start()
            if hop == LONG:
                value = term(dz, y)
                for way in (0, 1):
                    last = rs_lengths(dz)[way] - 1
                    rs_y(dz, way, last).wait_recv()
                    value = value + rs_recv[dz, way, last]
                if dz == 3:
                    rz_send[0] = value
                    rs_z(0).start()
                elif dz == 2:
                    rs_z(0).wait_recv()
                    rz_send[1] = value + rz_recv[0]
                    rs_z(1).start()
                elif dz == 1:
                    rz_send[2] = value
                    rs_z(2).start()
                else:
                    rs_z(2).wait_recv()
                    value = value + rz_recv[2]
                    rs_z(1).wait_recv()
                    out_ref[...] = value + rz_recv[1]

    for k in range(3):
        ag_z(k).wait_send()
        rs_z(k).wait_send()
    for dz in range(ZH):
        for way in (0, 1):
            for hop in range(ag_lengths(dz)[way]):
                ag_y(dz, way, hop).wait_send()
            for hop in range(rs_lengths(dz)[way]):
                rs_y(dz, way, hop).wait_send()
    for i, (tx, ty) in enumerate(tiles):
        at = window(codes, gx, gy)
        where = {"gx": tx, "gy": ty}
        remote(at, at, code_s.at[i], code_r.at[i], where).wait_send()
        remote(
            wown.at[pl.ds(first_level(tx, ty), 3)], window(field.at[0], gx, gy),
            t_s.at[i], t_r.at[i], where,
        ).wait_send()
        remote(
            window(field.at[0], tx, ty), back_at(back, gx, gy), b_s.at[i], b_r.at[i], where
        ).wait_send()
    for i, (dx, dy) in enumerate(offsets):
        sx, sy = tile_of(-dx, -dy)
        forward(i, sx, sy).wait_send()
    forward(len(offsets), gx, gy).wait_send()
    swap_p.wait_send()
    swap_w.wait_send()


def coefficients(gx_n, gy_n, offsets, tile_of, window, remote, codes, coef, code_s, code_r):
    for i, (dx, dy) in enumerate(offsets):
        sx, sy = tile_of(-dx, -dy)
        at = window(codes, sx, sy)
        remote(at, at, code_s.at[i], code_r.at[i], {"gx": sx, "gy": sy}).wait_recv()

    def lookup(code):
        return sum(TABLE[c] * (code == c).astype(F32) for c in range(4))

    cx, cy = lookup(codes[0]), lookup(codes[1])
    mask = jnp.where(codes[2] == 1, F32(1.0), F32(0.3))
    rows, cols = cx.shape
    row = lax.broadcasted_iota(jnp.int32, cx.shape, 0)
    col = lax.broadcasted_iota(jnp.int32, cx.shape, 1)
    zero = jnp.zeros_like(cx)
    east = jnp.where(row < rows - 1, 0.5 * (cx + pltpu.roll(cx, rows - 1, 0)), zero)
    west = jnp.where(row > 0, 0.5 * (cx + pltpu.roll(cx, 1, 0)), zero)
    north = jnp.where(col < cols - 1, 0.5 * (cy + pltpu.roll(cy, cols - 1, 1)), zero)
    south = jnp.where(col > 0, 0.5 * (cy + pltpu.roll(cy, 1, 1)), zero)
    coef[0] = mask * (1.0 - (east + west + north + south))
    coef[1] = east * pltpu.roll(mask, rows - 1, 0)
    coef[2] = west * pltpu.roll(mask, 1, 0)
    coef[3] = north * pltpu.roll(mask, cols - 1, 1)
    coef[4] = south * pltpu.roll(mask, 1, 1)
    coef[5] = mask * east
    coef[6] = mask * west
    coef[7] = mask * north
    coef[8] = mask * south


def solution(mesh):
    gx_n, gy_n = mesh.shape["gx"], mesh.shape["gy"]
    offsets = [(dx, dy) for dx in range(gx_n) for dy in range(gy_n) if (dx, dy) != (0, 0)]
    others = len(offsets)

    def per_device(gradient, perturbation, classes, land_sea):
        tile = gradient.shape[1:]
        grid = (tile[0] * gx_n, tile[1] * gy_n)
        three = (3,) + tile
        dma = pltpu.SemaphoreType.DMA
        any_space = pl.BlockSpec(memory_space=pl.ANY)
        return pl.pallas_call(
            functools.partial(kernel, gx_n, gy_n, offsets),
            out_shape=jax.ShapeDtypeStruct(three, F32),
            in_specs=[any_space] * 4,
            out_specs=pl.BlockSpec(memory_space=pltpu.VMEM),
            scratch_shapes=[
                pltpu.VMEM((BLOCKS,) + three, F32),
                pltpu.VMEM((BLOCKS,) + three, jnp.bfloat16),
                pltpu.VMEM((BLOCKS,) + three, jnp.bfloat16),
                pltpu.VMEM((BLOCKS,) + three, F32),
                pltpu.VMEM((BLOCKS,) + three, F32),
                pltpu.VMEM((3,) + grid, jnp.int32),
                pltpu.VMEM((9,) + grid, F32),
                pltpu.VMEM((LEVELS,) + tile, F32),
                pltpu.VMEM((LEVELS,) + tile, F32),
                pltpu.VMEM((LEVELS,) + tile, F32),
                pltpu.VMEM((2, 3) + grid, F32),
                pltpu.VMEM((gx_n, 3 * gy_n) + tile, F32),
                pltpu.VMEM((gx_n, 3 * gy_n) + tile, F32),
                pltpu.VMEM((LEVELS + 2,) + tile, F32),
                pltpu.VMEM((LEVELS + 2,) + tile, F32),
                pltpu.VMEM((ZH, 2, LONG) + three, F32),
                pltpu.VMEM((ZH, 2, LONG) + three, F32),
                pltpu.VMEM((3,) + three, F32),
                pltpu.VMEM((3,) + three, F32),
                dma((5,)),
                dma((3,)), dma((3,)),
                dma((ZH, 2, LONG)), dma((ZH, 2, LONG)),
                dma((others,)), dma((others,)),
                dma, dma, dma, dma,
                dma((others,)), dma((others,)),
                dma((others,)), dma((others,)),
                dma((others + 1,)), dma((others + 1,)),
                dma((ZH, 2, LONG)), dma((ZH, 2, LONG)),
                dma((3,)), dma((3,)),
            ],
            compiler_params=pltpu.CompilerParams(collective_id=0, has_side_effects=True),
        )(
            gradient,
            perturbation.reshape((BLOCKS, 2) + three),
            classes,
            land_sea.reshape((1,) + tile),
        )

    placed = (P("mem", "gx", "gy"), P("mem", None, "gx", "gy"), P(None, "gx", "gy"), P("gx", "gy"))
    return jax.shard_map(
        per_device, mesh=mesh, in_specs=placed, out_specs=P("mem", "gx", "gy"), check_vma=False
    )
```

```python
import functools

import jax
import jax.numpy as jnp
from jax import lax
from jax.experimental import pallas as pl
from jax.experimental.pallas import tpu as pltpu
from jax.sharding import PartitionSpec as P

LEVELS = 32
STEPS = 8
TABLE = (0.03, 0.07, 0.12, 0.18)
MESH = pl.DeviceIdType.MESH

ZH = 4
YN = 8
BLOCKS = ZH * YN
F32 = jnp.float32

HOPS = (1, 2, -1, -2, 1, 2, -1)
SOURCES = (-1, -2, 1, 2, -3, -4, 3)


def kernel(
    gx_n, gy_n, offsets,
    grad_hbm, pert_hbm, classes_hbm, sea_hbm, out_ref,
    gall, pown, praw, psend, pother, codes, coef,
    wsend, wrecv, wown, field, back, back_other, s_own, s_other,
    rs_send, rs_recv, rz_send, rz_recv,
    loc, agz_s, agz_r, agy_s, agy_r, code_s, code_r, px_s, px_r, w_s, w_r,
    t_s, t_r, b_s, b_r, fw_s, fw_r, rsy_s, rsy_r, rsz_s, rsz_r,
):
    mem = lax.axis_index("mem")
    gx = lax.axis_index("gx")
    gy = lax.axis_index("gy")
    core = lax.rem(mem, 2)
    y = lax.rem(mem // 2, YN)
    zh = mem // (2 * YN)

    def mem_at(z, yy):
        return {"mem": block(z, yy) * 2 + core}

    partner = {"mem": mem + 1 - 2 * core}

    def z_of(dz):
        return zh + (0, 1, -1, 2)[dz]

    def way(dz):
        return 1 if dz % 2 == 0 else -1

    def block(z, yy):
        return lax.rem(z + ZH, ZH) * YN + lax.rem(yy + YN, YN)

    def tile_of(dx, dy):
        return lax.rem(gx + dx + gx_n, gx_n), lax.rem(gy + dy + gy_n, gy_n)

    sent = []

    def remote(src, dst, ssem, rsem, where):
        return pltpu.make_async_remote_copy(
            src_ref=src, dst_ref=dst, send_sem=ssem, recv_sem=rsem,
            device_id=where, device_id_type=MESH,
        )

    def send(copy):
        copy.start()
        sent.append(copy)

    def window(ref, tx, ty):
        return ref.at[
            :, pl.ds(pl.multiple_of(tx * 16, 16), 16), pl.ds(pl.multiple_of(ty * 128, 128), 128)
        ]

    barrier = pltpu.get_barrier_semaphore()
    tiles = [tile_of(dx, dy) for dx, dy in offsets]
    near = [mem_at(zh, y + d) for d in (1, -1, 2, -2)] + [mem_at(z_of(dz), y) for dz in (1, 2, 3)]
    near.append(partner)
    for where in near:
        pl.semaphore_signal(barrier, inc=1, device_id=where, device_id_type=MESH)
    for tx, ty in tiles:
        pl.semaphore_signal(barrier, inc=1, device_id={"gx": tx, "gy": ty}, device_id_type=MESH)
    mine = block(zh, y)
    c_grad = pltpu.make_async_copy(grad_hbm, gall.at[mine], loc.at[0])
    c_cls = pltpu.make_async_copy(classes_hbm, window(codes, gx, gy).at[pl.ds(0, 2)], loc.at[1])
    c_sea = pltpu.make_async_copy(sea_hbm, window(codes, gx, gy).at[pl.ds(2, 1)], loc.at[2])
    c_raw = pltpu.make_async_copy(pert_hbm.at[:, 1 - core], praw, loc.at[3])
    c_own = pltpu.make_async_copy(pert_hbm.at[:, core], pown, loc.at[4])
    for copy in (c_grad, c_cls, c_sea, c_raw, c_own):
        copy.start()
    c_grad.wait()
    pl.semaphore_wait(barrier, len(near) + len(offsets))

    def ag_z(dz):
        at = gall.at[mine]
        return remote(at, at, agz_s.at[dz], agz_r.at[dz], mem_at(z_of(dz), y))

    def ag_z_in(dz):
        k = (0, 2, 1, 3)[dz]
        at = gall.at[block(z_of(dz), y)]
        return remote(at, at, agz_s.at[k], agz_r.at[k], mem_at(z_of(dz), y))

    def ag_y(dz, m):
        hop = HOPS[m] * way(dz)
        at = gall.at[block(z_of(dz), y + SOURCES[m] * way(dz) + hop)]
        return remote(at, at, agy_s.at[dz, m], agy_r.at[dz, m], mem_at(zh, y + hop))

    def ag_y_in(dz, m):
        hop = HOPS[m] * way(dz)
        at = gall.at[block(z_of(dz), y + SOURCES[m] * way(dz))]
        return remote(at, at, agy_s.at[dz, m], agy_r.at[dz, m], mem_at(zh, y - hop))

    def ag_first(dz):
        for m in (1, 3, 0, 2):
            send(ag_y(dz, m))

    def ag_second(dz):
        ag_y_in(dz, 1).wait_recv()
        send(ag_y(dz, 5))
        send(ag_y(dz, 4))
        ag_y_in(dz, 3).wait_recv()
        send(ag_y(dz, 6))

    for dz in (3, 1, 2):
        send(ag_z(dz))
    ag_first(0)

    c_cls.wait()
    c_sea.wait()
    for i, (tx, ty) in enumerate(tiles):
        at = window(codes, gx, gy)
        send(remote(at, at, code_s.at[i], code_r.at[i], {"gx": tx, "gy": ty}))
    c_raw.wait()

    @pl.loop(0, BLOCKS)
    def _(b):
        psend[b] = praw[b].astype(F32)

    swap_p = remote(psend, pother, px_s, px_r, partner)
    send(swap_p)
    c_own.wait()

    wown[...] = jnp.zeros_like(wown)
    wsend[...] = jnp.zeros_like(wsend)

    def add_up(dz, p_ref, w_ref):
        @pl.loop(0, YN, unroll=2)
        def _(yy):
            b = block(z_of(dz), yy)
            levels = pl.ds(lax.rem(6 * b + 3 * core, LEVELS), 3)
            w_ref[levels] = w_ref[levels] + p_ref[b].astype(F32) * gall[b]

    def ag_rest(dz):
        for m in (0, 2, 4, 6, 5):
            ag_y_in(dz, m).wait_recv()

    def wrap(w_ref):
        w_ref[pl.ds(0, 2)] = w_ref[pl.ds(0, 2)] + w_ref[pl.ds(LEVELS, 2)]

    ag_second(0)
    for dz in (1, 2, 3):
        ag_z_in(dz).wait_recv()
        ag_first(dz)
    ag_second(1)
    ag_second(2)
    swap_p.wait_recv()
    ag_rest(0)
    add_up(0, pother, wsend)
    add_up(0, pown, wown)
    ag_second(3)
    coefficients(offsets, tile_of, window, remote, codes, coef, code_s, code_r)
    for dz in (1, 2):
        ag_rest(dz)
        add_up(dz, pother, wsend)
        add_up(dz, pown, wown)
    ag_rest(3)
    add_up(3, pother, wsend)
    wrap(wsend)
    swap_w = remote(wsend, wrecv, w_s, w_r, partner)
    send(swap_w)
    add_up(3, pown, wown)
    wrap(wown)
    swap_w.wait_recv()
    wown[...] = wown[...] + wrecv[...]

    def first_level(tx, ty):
        return 8 * tx + jnp.minimum(3 * ty, 5)

    for i, (tx, ty) in enumerate(tiles):
        send(remote(
            wown.at[pl.ds(first_level(tx, ty), 3)], window(field.at[0], gx, gy),
            t_s.at[i], t_r.at[i], {"gx": tx, "gy": ty},
        ))
    c_field = pltpu.make_async_copy(
        wown.at[pl.ds(first_level(gx, gy), 3)], window(field.at[0], gx, gy), loc.at[0]
    )
    c_field.start()
    c_field.wait()
    for i, (dx, dy) in enumerate(offsets):
        sx, sy = tile_of(-dx, -dy)
        remote(
            wown.at[pl.ds(first_level(gx, gy), 3)], window(field.at[0], sx, sy),
            t_s.at[i], t_r.at[i], {"gx": sx, "gy": sy},
        ).wait_recv()

    def stencil(source, target, base):
        for lev in range(3):
            v = field[source, lev]
            rows, cols = v.shape
            field[target, lev] = (
                coef[0] * v
                + coef[base] * pltpu.roll(v, rows - 1, 0)
                + coef[base + 1] * pltpu.roll(v, 1, 0)
                + coef[base + 2] * pltpu.roll(v, cols - 1, 1)
                + coef[base + 3] * pltpu.roll(v, 1, 1)
            )

    for base in (1, 5):
        @pl.loop(0, STEPS // 2)
        def _(_):
            stencil(0, 1, base)
            stencil(1, 0, base)

    def back_at(ref, tx, ty):
        return ref.at[tx, pl.ds(3 * ty, 3)]

    for i, (tx, ty) in enumerate(tiles):
        send(remote(
            window(field.at[0], tx, ty), back_at(back, gx, gy), b_s.at[i], b_r.at[i],
            {"gx": tx, "gy": ty},
        ))
    c_back = pltpu.make_async_copy(window(field.at[0], gx, gy), back_at(back, gx, gy), loc.at[0])
    c_back.start()
    c_back.wait()

    def forward(i, tx, ty):
        return remote(
            back_at(back, tx, ty), back_at(back_other, tx, ty), fw_s.at[i], fw_r.at[i], partner
        )

    send(forward(len(offsets), gx, gy))
    for i, (dx, dy) in enumerate(offsets):
        sx, sy = tile_of(-dx, -dy)
        remote(
            window(field.at[0], sx, sy), back_at(back, sx, sy), b_s.at[i], b_r.at[i],
            {"gx": sx, "gy": sy},
        ).wait_recv()
        send(forward(i, sx, sy))

    def gathered(ref, s_ref):
        levels = jnp.concatenate([ref[:, 0:6], ref[:, 7:9]], axis=1) * F32(1.0 / 63.0)
        levels = levels.reshape((LEVELS,) + levels.shape[2:])
        s_ref[pl.ds(0, LEVELS)] = levels
        s_ref[pl.ds(LEVELS, 2)] = levels[0:2]

    gathered(back, s_own)
    for i, (dx, dy) in enumerate(offsets):
        sx, sy = tile_of(-dx, -dy)
        forward(i, sx, sy).wait_recv()
    forward(len(offsets), gx, gy).wait_recv()
    gathered(back_other, s_other)

    def term(dz, yy):
        b = block(z_of(dz), yy)
        levels = pl.ds(lax.rem(6 * b + 3 * core, LEVELS), 3)
        return pown[b].astype(F32) * s_own[levels] + pother[b] * s_other[levels]

    def rs_y(dz, m):
        return remote(
            rs_send.at[dz, m], rs_recv.at[dz, m], rsy_s.at[dz, m], rsy_r.at[dz, m],
            mem_at(zh, y + HOPS[m] * way(dz)),
        )

    def rs_put(dz, m, distance, parts=()):
        value = term(dz, y + distance * way(dz))
        for part in parts:
            rs_y(dz, part).wait_recv()
            value = value + rs_recv[dz, part]
        rs_send[dz, m] = value
        send(rs_y(dz, m))

    def rs_z(dz):
        return remote(
            rz_send.at[dz], rz_recv.at[dz], rsz_s.at[dz], rsz_r.at[dz], mem_at(z_of(dz), y)
        )

    order = (3, 1, 2, 0)
    for dz in order:
        rs_put(dz, 5, 4)
        rs_put(dz, 4, 3)
        rs_put(dz, 6, -3)
    for dz in order:
        rs_put(dz, 0, 1)
        rs_put(dz, 2, -1)
        rs_put(dz, 1, 2, (4, 5))
        rs_put(dz, 3, -2, (6,))
    for dz in order:
        value = term(dz, y)
        for m in (0, 2, 1, 3):
            rs_y(dz, m).wait_recv()
            value = value + rs_recv[dz, m]
        if dz == 0:
            for k in (1, 2, 3):
                rs_z(k).wait_recv()
                value = value + rz_recv[k]
            out_ref[...] = value
        else:
            rz_send[dz] = value
            send(rs_z(dz))

    for copy in sent:
        copy.wait_send()


def coefficients(offsets, tile_of, window, remote, codes, coef, code_s, code_r):
    for i, (dx, dy) in enumerate(offsets):
        sx, sy = tile_of(-dx, -dy)
        at = window(codes, sx, sy)
        remote(at, at, code_s.at[i], code_r.at[i], {"gx": sx, "gy": sy}).wait_recv()

    def lookup(code):
        return sum(TABLE[c] * (code == c).astype(F32) for c in range(4))

    cx, cy = lookup(codes[0]), lookup(codes[1])
    mask = jnp.where(codes[2] == 1, F32(1.0), F32(0.3))
    rows, cols = cx.shape
    row = lax.broadcasted_iota(jnp.int32, cx.shape, 0)
    col = lax.broadcasted_iota(jnp.int32, cx.shape, 1)
    zero = jnp.zeros_like(cx)
    east = jnp.where(row < rows - 1, 0.5 * (cx + pltpu.roll(cx, rows - 1, 0)), zero)
    west = jnp.where(row > 0, 0.5 * (cx + pltpu.roll(cx, 1, 0)), zero)
    north = jnp.where(col < cols - 1, 0.5 * (cy + pltpu.roll(cy, cols - 1, 1)), zero)
    south = jnp.where(col > 0, 0.5 * (cy + pltpu.roll(cy, 1, 1)), zero)
    coef[0] = mask * (1.0 - (east + west + north + south))
    coef[1] = east * pltpu.roll(mask, rows - 1, 0)
    coef[2] = west * pltpu.roll(mask, 1, 0)
    coef[3] = north * pltpu.roll(mask, cols - 1, 1)
    coef[4] = south * pltpu.roll(mask, 1, 1)
    coef[5] = mask * east
    coef[6] = mask * west
    coef[7] = mask * north
    coef[8] = mask * south


def solution(mesh):
    gx_n, gy_n = mesh.shape["gx"], mesh.shape["gy"]
    offsets = [(dx, dy) for dx in range(gx_n) for dy in range(gy_n) if (dx, dy) != (0, 0)]
    others = len(offsets)

    def per_device(gradient, perturbation, classes, land_sea):
        tile = gradient.shape[1:]
        grid = (tile[0] * gx_n, tile[1] * gy_n)
        three = (3,) + tile
        dma = pltpu.SemaphoreType.DMA
        any_space = pl.BlockSpec(memory_space=pl.ANY)
        return pl.pallas_call(
            functools.partial(kernel, gx_n, gy_n, offsets),
            out_shape=jax.ShapeDtypeStruct(three, F32),
            in_specs=[any_space] * 4,
            out_specs=pl.BlockSpec(memory_space=pltpu.VMEM),
            scratch_shapes=[
                pltpu.VMEM((BLOCKS,) + three, F32),
                pltpu.VMEM((BLOCKS,) + three, jnp.bfloat16),
                pltpu.VMEM((BLOCKS,) + three, jnp.bfloat16),
                pltpu.VMEM((BLOCKS,) + three, F32),
                pltpu.VMEM((BLOCKS,) + three, F32),
                pltpu.VMEM((3,) + grid, jnp.int32),
                pltpu.VMEM((9,) + grid, F32),
                pltpu.VMEM((LEVELS + 2,) + tile, F32),
                pltpu.VMEM((LEVELS + 2,) + tile, F32),
                pltpu.VMEM((LEVELS + 2,) + tile, F32),
                pltpu.VMEM((2, 3) + grid, F32),
                pltpu.VMEM((gx_n, 3 * gy_n) + tile, F32),
                pltpu.VMEM((gx_n, 3 * gy_n) + tile, F32),
                pltpu.VMEM((LEVELS + 2,) + tile, F32),
                pltpu.VMEM((LEVELS + 2,) + tile, F32),
                pltpu.VMEM((ZH, 7) + three, F32),
                pltpu.VMEM((ZH, 7) + three, F32),
                pltpu.VMEM((ZH,) + three, F32),
                pltpu.VMEM((ZH,) + three, F32),
                dma((5,)),
                dma((ZH,)), dma((ZH,)),
                dma((ZH, 7)), dma((ZH, 7)),
                dma((others,)), dma((others,)),
                dma, dma, dma, dma,
                dma((others,)), dma((others,)),
                dma((others,)), dma((others,)),
                dma((others + 1,)), dma((others + 1,)),
                dma((ZH, 7)), dma((ZH, 7)),
                dma((ZH,)), dma((ZH,)),
            ],
            compiler_params=pltpu.CompilerParams(collective_id=0, has_side_effects=True),
        )(
            gradient,
            perturbation.reshape((BLOCKS, 2) + three),
            classes,
            land_sea.reshape((1,) + tile),
        )

    placed = (P("mem", "gx", "gy"), P("mem", None, "gx", "gy"), P(None, "gx", "gy"), P("gx", "gy"))
    return jax.shard_map(
        per_device, mesh=mesh, in_specs=placed, out_specs=P("mem", "gx", "gy"), check_vma=False
    )
```

```python
import functools

import jax
import jax.numpy as jnp
from jax import lax
from jax.experimental import pallas as pl
from jax.experimental.pallas import tpu as pltpu
from jax.sharding import PartitionSpec as P

LEVELS = 32
STEPS = 8
TABLE = (0.03, 0.07, 0.12, 0.18)
MESH = pl.DeviceIdType.MESH

ZH = 4
YN = 8
BLOCKS = ZH * YN
F32 = jnp.float32

HOPS = (1, 2, -1, -2, 1, 2, -1)
SOURCES = (-1, -2, 1, 2, -3, -4, 3)


def kernel(
    gx_n, gy_n, offsets,
    grad_hbm, pert_hbm, classes_hbm, sea_hbm, out_ref,
    gall, pown, praw, psend, pother, codes, coef,
    wsend, wrecv, wown, field, back, back_other, s_own, s_other,
    rs_send, rs_recv, rz_send, rz_recv,
    loc, agz_s, agz_r, agy_s, agy_r, code_s, code_r, px_s, px_r, w_s, w_r,
    t_s, t_r, b_s, b_r, fw_s, fw_r, rsy_s, rsy_r, rsz_s, rsz_r,
):
    mem = lax.axis_index("mem")
    gx = lax.axis_index("gx")
    gy = lax.axis_index("gy")
    core = lax.rem(mem, 2)
    y = lax.rem(mem // 2, YN)
    zh = mem // (2 * YN)

    def mem_at(z, yy):
        return {"mem": block(z, yy) * 2 + core}

    partner = {"mem": mem + 1 - 2 * core}

    def z_of(dz):
        return zh + (0, 1, -1, 2)[dz]

    def way(dz):
        return 1 if dz % 2 == 0 else -1

    def block(z, yy):
        return lax.rem(z + ZH, ZH) * YN + lax.rem(yy + YN, YN)

    def tile_of(dx, dy):
        return lax.rem(gx + dx + gx_n, gx_n), lax.rem(gy + dy + gy_n, gy_n)

    sent = []

    def remote(src, dst, ssem, rsem, where):
        return pltpu.make_async_remote_copy(
            src_ref=src, dst_ref=dst, send_sem=ssem, recv_sem=rsem,
            device_id=where, device_id_type=MESH,
        )

    def send(copy):
        copy.start()
        sent.append(copy)

    def window(ref, tx, ty):
        return ref.at[
            :, pl.ds(pl.multiple_of(tx * 16, 16), 16), pl.ds(pl.multiple_of(ty * 128, 128), 128)
        ]

    barrier = pltpu.get_barrier_semaphore()
    tiles = [tile_of(dx, dy) for dx, dy in offsets]
    near = [mem_at(zh, y + d) for d in (1, -1, 2, -2)] + [mem_at(z_of(dz), y) for dz in (1, 2, 3)]
    near.append(partner)
    for where in near:
        pl.semaphore_signal(barrier, inc=1, device_id=where, device_id_type=MESH)
    for tx, ty in tiles:
        pl.semaphore_signal(barrier, inc=1, device_id={"gx": tx, "gy": ty}, device_id_type=MESH)
    mine = block(zh, y)
    c_grad = pltpu.make_async_copy(grad_hbm, gall.at[mine], loc.at[0])
    c_cls = pltpu.make_async_copy(classes_hbm, window(codes, gx, gy).at[pl.ds(0, 2)], loc.at[1])
    c_sea = pltpu.make_async_copy(sea_hbm, window(codes, gx, gy).at[pl.ds(2, 1)], loc.at[2])
    c_raw = pltpu.make_async_copy(pert_hbm.at[:, 1 - core], praw, loc.at[3])
    c_own = pltpu.make_async_copy(pert_hbm.at[:, core], pown, loc.at[4])
    for copy in (c_grad, c_cls, c_sea, c_raw, c_own):
        copy.start()
    c_grad.wait()
    pl.semaphore_wait(barrier, len(near) + len(offsets))

    def ag_z(dz):
        at = gall.at[mine]
        return remote(at, at, agz_s.at[dz], agz_r.at[dz], mem_at(z_of(dz), y))

    def ag_z_in(dz):
        k = (0, 2, 1, 3)[dz]
        at = gall.at[block(z_of(dz), y)]
        return remote(at, at, agz_s.at[k], agz_r.at[k], mem_at(z_of(dz), y))

    def ag_y(dz, m):
        hop = HOPS[m] * way(dz)
        at = gall.at[block(z_of(dz), y + SOURCES[m] * way(dz) + hop)]
        return remote(at, at, agy_s.at[dz, m], agy_r.at[dz, m], mem_at(zh, y + hop))

    def ag_y_in(dz, m):
        hop = HOPS[m] * way(dz)
        at = gall.at[block(z_of(dz), y + SOURCES[m] * way(dz))]
        return remote(at, at, agy_s.at[dz, m], agy_r.at[dz, m], mem_at(zh, y - hop))

    def ag_first(dz):
        for m in (1, 3, 0, 2):
            send(ag_y(dz, m))

    def ag_second(dz):
        ag_y_in(dz, 1).wait_recv()
        send(ag_y(dz, 5))
        send(ag_y(dz, 4))
        ag_y_in(dz, 3).wait_recv()
        send(ag_y(dz, 6))

    for dz in (3, 1, 2):
        send(ag_z(dz))
    ag_first(0)

    c_cls.wait()
    c_sea.wait()
    for i, (tx, ty) in enumerate(tiles):
        at = window(codes, gx, gy)
        send(remote(at, at, code_s.at[i], code_r.at[i], {"gx": tx, "gy": ty}))
    c_raw.wait()

    @pl.loop(0, BLOCKS)
    def _(b):
        psend[b] = praw[b].astype(F32)

    swap_p = remote(psend, pother, px_s, px_r, partner)
    send(swap_p)
    c_own.wait()

    wown[...] = jnp.zeros_like(wown)
    wsend[...] = jnp.zeros_like(wsend)

    def add_up(dz, p_ref, w_ref):
        @pl.loop(0, YN, unroll=2)
        def _(yy):
            b = block(z_of(dz), yy)
            levels = pl.ds(lax.rem(6 * b + 3 * core, LEVELS), 3)
            w_ref[levels] = w_ref[levels] + p_ref[b].astype(F32) * gall[b]

    def ag_rest(dz):
        for m in (0, 2, 4, 6, 5):
            ag_y_in(dz, m).wait_recv()

    def wrap(w_ref):
        w_ref[pl.ds(0, 2)] = w_ref[pl.ds(0, 2)] + w_ref[pl.ds(LEVELS, 2)]

    ag_second(0)
    for dz in (1, 2, 3):
        ag_z_in(dz).wait_recv()
        ag_first(dz)
    ag_second(1)
    ag_second(2)
    swap_p.wait_recv()
    ag_rest(0)
    add_up(0, pother, wsend)
    add_up(0, pown, wown)
    ag_second(3)
    coefficients(offsets, tile_of, window, remote, codes, coef, code_s, code_r)
    for dz in (1, 2):
        ag_rest(dz)
        add_up(dz, pother, wsend)
        add_up(dz, pown, wown)
    ag_rest(3)
    add_up(3, pother, wsend)
    wrap(wsend)
    swap_w = remote(wsend, wrecv, w_s, w_r, partner)
    send(swap_w)
    add_up(3, pown, wown)
    wrap(wown)
    swap_w.wait_recv()
    wown[...] = wown[...] + wrecv[...]

    def first_level(tx, ty):
        return 8 * tx + jnp.minimum(3 * ty, 5)

    for i, (tx, ty) in enumerate(tiles):
        send(remote(
            wown.at[pl.ds(first_level(tx, ty), 3)], window(field.at[0], gx, gy),
            t_s.at[i], t_r.at[i], {"gx": tx, "gy": ty},
        ))
    c_field = pltpu.make_async_copy(
        wown.at[pl.ds(first_level(gx, gy), 3)], window(field.at[0], gx, gy), loc.at[0]
    )
    c_field.start()
    c_field.wait()
    for i, (dx, dy) in enumerate(offsets):
        sx, sy = tile_of(-dx, -dy)
        remote(
            wown.at[pl.ds(first_level(gx, gy), 3)], window(field.at[0], sx, sy),
            t_s.at[i], t_r.at[i], {"gx": sx, "gy": sy},
        ).wait_recv()

    def stencil(source, target, base):
        for lev in range(3):
            v = field[source, lev]
            rows, cols = v.shape
            field[target, lev] = (
                coef[0] * v
                + coef[base] * pltpu.roll(v, rows - 1, 0)
                + coef[base + 1] * pltpu.roll(v, 1, 0)
                + coef[base + 2] * pltpu.roll(v, cols - 1, 1)
                + coef[base + 3] * pltpu.roll(v, 1, 1)
            )

    for base in (1, 5):
        @pl.loop(0, STEPS // 2)
        def _(_):
            stencil(0, 1, base)
            stencil(1, 0, base)

    def back_at(ref, tx, ty):
        return ref.at[tx, pl.ds(3 * ty, 3)]

    for i, (tx, ty) in enumerate(tiles):
        send(remote(
            window(field.at[0], tx, ty), back_at(back, gx, gy), b_s.at[i], b_r.at[i],
            {"gx": tx, "gy": ty},
        ))
    c_back = pltpu.make_async_copy(window(field.at[0], gx, gy), back_at(back, gx, gy), loc.at[0])
    c_back.start()
    c_back.wait()

    def forward(i, tx, ty):
        return remote(
            back_at(back, tx, ty), back_at(back_other, tx, ty), fw_s.at[i], fw_r.at[i], partner
        )

    send(forward(len(offsets), gx, gy))
    for i, (dx, dy) in enumerate(offsets):
        sx, sy = tile_of(-dx, -dy)
        remote(
            window(field.at[0], sx, sy), back_at(back, sx, sy), b_s.at[i], b_r.at[i],
            {"gx": sx, "gy": sy},
        ).wait_recv()
        send(forward(i, sx, sy))

    def gathered(ref, s_ref):
        levels = jnp.concatenate([ref[:, 0:6], ref[:, 7:9]], axis=1) * F32(1.0 / 63.0)
        levels = levels.reshape((LEVELS,) + levels.shape[2:])
        s_ref[pl.ds(0, LEVELS)] = levels
        s_ref[pl.ds(LEVELS, 2)] = levels[0:2]

    gathered(back, s_own)
    for i, (dx, dy) in enumerate(offsets):
        sx, sy = tile_of(-dx, -dy)
        forward(i, sx, sy).wait_recv()
    forward(len(offsets), gx, gy).wait_recv()
    gathered(back_other, s_other)

    def term(dz, yy):
        b = block(z_of(dz), yy)
        levels = pl.ds(lax.rem(6 * b + 3 * core, LEVELS), 3)
        return pown[b].astype(F32) * s_own[levels] + pother[b] * s_other[levels]

    def rs_y(dz, m):
        return remote(
            rs_send.at[dz, m], rs_recv.at[dz, m], rsy_s.at[dz, m], rsy_r.at[dz, m],
            mem_at(zh, y + HOPS[m] * way(dz)),
        )

    def rs_put(dz, m, distance, parts=()):
        value = term(dz, y + distance * way(dz))
        for part in parts:
            rs_y(dz, part).wait_recv()
            value = value + rs_recv[dz, part]
        rs_send[dz, m] = value
        send(rs_y(dz, m))

    def rs_z(dz):
        return remote(
            rz_send.at[dz], rz_recv.at[dz], rsz_s.at[dz], rsz_r.at[dz], mem_at(z_of(dz), y)
        )

    order = (3, 1, 2, 0)
    for dz in order:
        rs_put(dz, 5, 4)
        rs_put(dz, 4, 3)
        rs_put(dz, 6, -3)
    for dz in order:
        rs_put(dz, 0, 1)
        rs_put(dz, 2, -1)
        rs_put(dz, 1, 2, (4, 5))
        rs_put(dz, 3, -2, (6,))
    for dz in order:
        value = term(dz, y)
        for m in (0, 2, 1, 3):
            rs_y(dz, m).wait_recv()
            value = value + rs_recv[dz, m]
        if dz == 0:
            for k in (1, 2, 3):
                rs_z(k).wait_recv()
                value = value + rz_recv[k]
            out_ref[...] = value
        else:
            rz_send[dz] = value
            send(rs_z(dz))

    for copy in sent:
        copy.wait_send()


def coefficients(offsets, tile_of, window, remote, codes, coef, code_s, code_r):
    for i, (dx, dy) in enumerate(offsets):
        sx, sy = tile_of(-dx, -dy)
        at = window(codes, sx, sy)
        remote(at, at, code_s.at[i], code_r.at[i], {"gx": sx, "gy": sy}).wait_recv()

    def lookup(code):
        return sum(TABLE[c] * (code == c).astype(F32) for c in range(4))

    cx, cy = lookup(codes[0]), lookup(codes[1])
    mask = jnp.where(codes[2] == 1, F32(1.0), F32(0.3))
    rows, cols = cx.shape
    row = lax.broadcasted_iota(jnp.int32, cx.shape, 0)
    col = lax.broadcasted_iota(jnp.int32, cx.shape, 1)
    zero = jnp.zeros_like(cx)
    east = jnp.where(row < rows - 1, 0.5 * (cx + pltpu.roll(cx, rows - 1, 0)), zero)
    west = jnp.where(row > 0, 0.5 * (cx + pltpu.roll(cx, 1, 0)), zero)
    north = jnp.where(col < cols - 1, 0.5 * (cy + pltpu.roll(cy, cols - 1, 1)), zero)
    south = jnp.where(col > 0, 0.5 * (cy + pltpu.roll(cy, 1, 1)), zero)
    coef[0] = mask * (1.0 - (east + west + north + south))
    coef[1] = east * pltpu.roll(mask, rows - 1, 0)
    coef[2] = west * pltpu.roll(mask, 1, 0)
    coef[3] = north * pltpu.roll(mask, cols - 1, 1)
    coef[4] = south * pltpu.roll(mask, 1, 1)
    coef[5] = mask * east
    coef[6] = mask * west
    coef[7] = mask * north
    coef[8] = mask * south


def solution(mesh):
    gx_n, gy_n = mesh.shape["gx"], mesh.shape["gy"]
    offsets = [(dx, dy) for dx in (2, 1, 3, 0) for dy in range(1, gy_n)]
    offsets += [(dx, 0) for dx in (2, 1, 3)]
    others = len(offsets)

    def per_device(gradient, perturbation, classes, land_sea):
        tile = gradient.shape[1:]
        grid = (tile[0] * gx_n, tile[1] * gy_n)
        three = (3,) + tile
        dma = pltpu.SemaphoreType.DMA
        any_space = pl.BlockSpec(memory_space=pl.ANY)
        return pl.pallas_call(
            functools.partial(kernel, gx_n, gy_n, offsets),
            out_shape=jax.ShapeDtypeStruct(three, F32),
            in_specs=[any_space] * 4,
            out_specs=pl.BlockSpec(memory_space=pltpu.VMEM),
            scratch_shapes=[
                pltpu.VMEM((BLOCKS,) + three, F32),
                pltpu.VMEM((BLOCKS,) + three, jnp.bfloat16),
                pltpu.VMEM((BLOCKS,) + three, jnp.bfloat16),
                pltpu.VMEM((BLOCKS,) + three, F32),
                pltpu.VMEM((BLOCKS,) + three, F32),
                pltpu.VMEM((3,) + grid, jnp.int32),
                pltpu.VMEM((9,) + grid, F32),
                pltpu.VMEM((LEVELS + 2,) + tile, F32),
                pltpu.VMEM((LEVELS + 2,) + tile, F32),
                pltpu.VMEM((LEVELS + 2,) + tile, F32),
                pltpu.VMEM((2, 3) + grid, F32),
                pltpu.VMEM((gx_n, 3 * gy_n) + tile, F32),
                pltpu.VMEM((gx_n, 3 * gy_n) + tile, F32),
                pltpu.VMEM((LEVELS + 2,) + tile, F32),
                pltpu.VMEM((LEVELS + 2,) + tile, F32),
                pltpu.VMEM((ZH, 7) + three, F32),
                pltpu.VMEM((ZH, 7) + three, F32),
                pltpu.VMEM((ZH,) + three, F32),
                pltpu.VMEM((ZH,) + three, F32),
                dma((5,)),
                dma((ZH,)), dma((ZH,)),
                dma((ZH, 7)), dma((ZH, 7)),
                dma((others,)), dma((others,)),
                dma, dma, dma, dma,
                dma((others,)), dma((others,)),
                dma((others,)), dma((others,)),
                dma((others + 1,)), dma((others + 1,)),
                dma((ZH, 7)), dma((ZH, 7)),
                dma((ZH,)), dma((ZH,)),
            ],
            compiler_params=pltpu.CompilerParams(collective_id=0, has_side_effects=True),
        )(
            gradient,
            perturbation.reshape((BLOCKS, 2) + three),
            classes,
            land_sea.reshape((1,) + tile),
        )

    placed = (P("mem", "gx", "gy"), P("mem", None, "gx", "gy"), P(None, "gx", "gy"), P("gx", "gy"))
    return jax.shard_map(
        per_device, mesh=mesh, in_specs=placed, out_specs=P("mem", "gx", "gy"), check_vma=False
    )
```

```python
import functools

import jax
import jax.numpy as jnp
from jax import lax
from jax.experimental import pallas as pl
from jax.experimental.pallas import tpu as pltpu
from jax.sharding import PartitionSpec as P

LEVELS = 32
STEPS = 8
TABLE = (0.03, 0.07, 0.12, 0.18)
MESH = pl.DeviceIdType.MESH

ZH = 4
YN = 8
BLOCKS = ZH * YN
F32 = jnp.float32

GROUPS = ((0, 1), (1, 2))
HOPS = (1, 2, -1, -2, 1, 2, -1)
SOURCES = (-1, -2, 1, 2, -3, -4, 3)


def kernel(
    gx_n, gy_n, offsets,
    grad_hbm, pert_hbm, classes_hbm, sea_hbm, out_ref,
    gall, pown, praw, psend, pother, codes, coef,
    wsend, wrecv, wown, field, back, back_other, s_own, s_other,
    rs_send, rs_recv, rz_send, rz_recv,
    loc, agz_s, agz_r, agy_s, agy_r, code_s, code_r, px_s, px_r, w_s, w_r,
    t_s, t_r, b_s, b_r, fw_s, fw_r, rsy_s, rsy_r, rsz_s, rsz_r,
):
    mem = lax.axis_index("mem")
    gx = lax.axis_index("gx")
    gy = lax.axis_index("gy")
    core = lax.rem(mem, 2)
    y = lax.rem(mem // 2, YN)
    zh = mem // (2 * YN)

    def mem_at(z, yy):
        return {"mem": block(z, yy) * 2 + core}

    partner = {"mem": mem + 1 - 2 * core}

    def z_of(dz):
        return zh + (0, 1, -1, 2)[dz]

    def way(dz):
        return 1 if dz % 2 == 0 else -1

    def block(z, yy):
        return lax.rem(z + ZH, ZH) * YN + lax.rem(yy + YN, YN)

    def tile_of(dx, dy):
        return lax.rem(gx + dx + gx_n, gx_n), lax.rem(gy + dy + gy_n, gy_n)

    sent = []

    def remote(src, dst, ssem, rsem, where):
        return pltpu.make_async_remote_copy(
            src_ref=src, dst_ref=dst, send_sem=ssem, recv_sem=rsem,
            device_id=where, device_id_type=MESH,
        )

    def send(copy):
        copy.start()
        sent.append(copy)

    def window(ref, tx, ty):
        return ref.at[
            :, pl.ds(pl.multiple_of(tx * 16, 16), 16), pl.ds(pl.multiple_of(ty * 128, 128), 128)
        ]

    barrier = pltpu.get_barrier_semaphore()
    tiles = [tile_of(dx, dy) for dx, dy in offsets]
    near = [mem_at(zh, y + d) for d in (1, -1, 2, -2)] + [mem_at(z_of(dz), y) for dz in (1, 2, 3)]
    near.append(partner)
    for where in near:
        pl.semaphore_signal(barrier, inc=1, device_id=where, device_id_type=MESH)
    for tx, ty in tiles:
        pl.semaphore_signal(barrier, inc=1, device_id={"gx": tx, "gy": ty}, device_id_type=MESH)
    mine = block(zh, y)
    c_grad = pltpu.make_async_copy(grad_hbm, gall.at[mine], loc.at[0])
    c_cls = pltpu.make_async_copy(classes_hbm, window(codes, gx, gy).at[pl.ds(0, 2)], loc.at[1])
    c_sea = pltpu.make_async_copy(sea_hbm, window(codes, gx, gy).at[pl.ds(2, 1)], loc.at[2])
    c_raw = pltpu.make_async_copy(pert_hbm.at[:, 1 - core], praw, loc.at[3])
    c_own = pltpu.make_async_copy(pert_hbm.at[:, core], pown, loc.at[4])
    for copy in (c_grad, c_cls, c_sea, c_raw, c_own):
        copy.start()
    c_grad.wait()
    pl.semaphore_wait(barrier, len(near) + len(offsets))

    def ag_z(dz):
        at = gall.at[mine]
        return remote(at, at, agz_s.at[dz], agz_r.at[dz], mem_at(z_of(dz), y))

    def ag_z_in(dz):
        k = (0, 2, 1, 3)[dz]
        at = gall.at[block(z_of(dz), y)]
        return remote(at, at, agz_s.at[k], agz_r.at[k], mem_at(z_of(dz), y))

    def ag_y(dz, m):
        hop = HOPS[m] * way(dz)
        at = gall.at[block(z_of(dz), y + SOURCES[m] * way(dz) + hop)]
        return remote(at, at, agy_s.at[dz, m], agy_r.at[dz, m], mem_at(zh, y + hop))

    def ag_y_in(dz, m):
        hop = HOPS[m] * way(dz)
        at = gall.at[block(z_of(dz), y + SOURCES[m] * way(dz))]
        return remote(at, at, agy_s.at[dz, m], agy_r.at[dz, m], mem_at(zh, y - hop))

    def ag_first(dz):
        for m in (1, 3, 0, 2):
            send(ag_y(dz, m))

    def ag_second(dz):
        ag_y_in(dz, 1).wait_recv()
        send(ag_y(dz, 5))
        send(ag_y(dz, 4))
        ag_y_in(dz, 3).wait_recv()
        send(ag_y(dz, 6))

    for dz in (3, 1, 2):
        send(ag_z(dz))
    ag_first(0)

    c_cls.wait()
    c_sea.wait()
    for i, (tx, ty) in enumerate(tiles):
        at = window(codes, gx, gy)
        send(remote(at, at, code_s.at[i], code_r.at[i], {"gx": tx, "gy": ty}))
    c_raw.wait()

    @pl.loop(0, BLOCKS)
    def _(b):
        psend[b] = praw[b].astype(F32)

    swap_p = remote(psend, pother, px_s, px_r, partner)
    send(swap_p)
    c_own.wait()

    wown[...] = jnp.zeros_like(wown)
    wsend[...] = jnp.zeros_like(wsend)

    def add_up(dz, p_ref, w_ref):
        @pl.loop(0, YN, unroll=2)
        def _(yy):
            b = block(z_of(dz), yy)
            levels = pl.ds(lax.rem(6 * b + 3 * core, LEVELS), 3)
            w_ref[levels] = w_ref[levels] + p_ref[b].astype(F32) * gall[b]

    def ag_rest(dz):
        for m in (0, 2, 4, 6, 5):
            ag_y_in(dz, m).wait_recv()

    def wrap(w_ref):
        w_ref[pl.ds(0, 2)] = w_ref[pl.ds(0, 2)] + w_ref[pl.ds(LEVELS, 2)]

    ag_second(0)
    for dz in (1, 2, 3):
        ag_z_in(dz).wait_recv()
        ag_first(dz)
    ag_second(1)
    ag_second(2)
    swap_p.wait_recv()
    ag_rest(0)
    add_up(0, pother, wsend)
    add_up(0, pown, wown)
    ag_second(3)
    coefficients(offsets, tile_of, window, remote, codes, coef, code_s, code_r)
    for dz in (1, 2):
        ag_rest(dz)
        add_up(dz, pother, wsend)
        add_up(dz, pown, wown)
    ag_rest(3)
    add_up(3, pother, wsend)
    wrap(wsend)
    swap_w = remote(wsend, wrecv, w_s, w_r, partner)
    send(swap_w)
    add_up(3, pown, wown)
    wrap(wown)
    swap_w.wait_recv()
    wown[...] = wown[...] + wrecv[...]

    def first_level(tx, ty):
        return 8 * tx + jnp.minimum(3 * ty, 5)

    def level_out(g, i, tx, ty):
        at, n = GROUPS[g]
        return remote(
            wown.at[pl.ds(first_level(tx, ty) + at, n)],
            window(field.at[0], gx, gy).at[pl.ds(at, n)],
            t_s.at[g, i], t_r.at[g, i], {"gx": tx, "gy": ty},
        )

    def level_back(g, i, tx, ty):
        at, n = GROUPS[g]
        return remote(
            window(field.at[0], tx, ty).at[pl.ds(at, n)],
            back.at[gx, pl.ds(3 * gy + at, n)],
            b_s.at[g, i], b_r.at[g, i], {"gx": tx, "gy": ty},
        )

    def forward(i, tx, ty):
        at = pl.ds(3 * ty, 3)
        return remote(back.at[tx, at], back_other.at[tx, at], fw_s.at[i], fw_r.at[i], partner)

    c_field = pltpu.make_async_copy(
        wown.at[pl.ds(first_level(gx, gy), 3)], window(field.at[0], gx, gy), loc.at[0]
    )
    c_field.start()
    for g in range(len(GROUPS)):
        for i, (tx, ty) in enumerate(tiles):
            send(level_out(g, i, tx, ty))
    c_field.wait()
    sources = [tile_of(-dx, -dy) for dx, dy in offsets]

    def step(v, base):
        rows, cols = v.shape
        return (
            coef[0] * v
            + coef[base] * pltpu.roll(v, rows - 1, 0)
            + coef[base + 1] * pltpu.roll(v, 1, 0)
            + coef[base + 2] * pltpu.roll(v, cols - 1, 1)
            + coef[base + 3] * pltpu.roll(v, 1, 1)
        )

    for g in range(len(GROUPS)):
        for i in range(len(offsets)):
            level_out(g, i, gx, gy).wait_recv()
        at, n = GROUPS[g]
        for base in (1, 5):
            @pl.loop(0, STEPS // 2)
            def _(_):
                for lev in range(at, at + n):
                    field[1, lev] = step(field[0, lev], base)
                for lev in range(at, at + n):
                    field[0, lev] = step(field[1, lev], base)
        for i, (tx, ty) in enumerate(tiles):
            send(level_back(g, i, tx, ty))
    c_back = pltpu.make_async_copy(
        window(field.at[0], gx, gy), back.at[gx, pl.ds(3 * gy, 3)], loc.at[0],
    )
    c_back.start()
    c_back.wait()
    send(forward(len(offsets), gx, gy))
    last = len(GROUPS) - 1
    for g in range(len(GROUPS)):
        for i, (sx, sy) in enumerate(sources):
            level_back(g, i, sx, sy).wait_recv()
            if g == last:
                send(forward(i, sx, sy))

    def gathered(ref, s_ref):
        levels = jnp.concatenate([ref[:, 0:6], ref[:, 7:9]], axis=1) * F32(1.0 / 63.0)
        levels = levels.reshape((LEVELS,) + levels.shape[2:])
        s_ref[pl.ds(0, LEVELS)] = levels
        s_ref[pl.ds(LEVELS, 2)] = levels[0:2]

    gathered(back, s_own)
    for i, (sx, sy) in enumerate(sources + [(gx, gy)]):
        forward(i, sx, sy).wait_recv()
    gathered(back_other, s_other)

    def term(dz, yy):
        b = block(z_of(dz), yy)
        levels = pl.ds(lax.rem(6 * b + 3 * core, LEVELS), 3)
        return pown[b].astype(F32) * s_own[levels] + pother[b] * s_other[levels]

    def rs_y(dz, m):
        return remote(
            rs_send.at[dz, m], rs_recv.at[dz, m], rsy_s.at[dz, m], rsy_r.at[dz, m],
            mem_at(zh, y + HOPS[m] * way(dz)),
        )

    def rs_put(dz, m, distance, parts=()):
        value = term(dz, y + distance * way(dz))
        for part in parts:
            rs_y(dz, part).wait_recv()
            value = value + rs_recv[dz, part]
        rs_send[dz, m] = value
        send(rs_y(dz, m))

    def rs_z(dz):
        return remote(
            rz_send.at[dz], rz_recv.at[dz], rsz_s.at[dz], rsz_r.at[dz], mem_at(z_of(dz), y)
        )

    order = (3, 1, 2, 0)
    for dz in order:
        rs_put(dz, 5, 4)
        rs_put(dz, 4, 3)
        rs_put(dz, 6, -3)
    for dz in order:
        rs_put(dz, 0, 1)
        rs_put(dz, 2, -1)
        rs_put(dz, 1, 2, (4, 5))
        rs_put(dz, 3, -2, (6,))
    for dz in order:
        value = term(dz, y)
        for m in (0, 2, 1, 3):
            rs_y(dz, m).wait_recv()
            value = value + rs_recv[dz, m]
        if dz == 0:
            for k in (1, 2, 3):
                rs_z(k).wait_recv()
                value = value + rz_recv[k]
            out_ref[...] = value
        else:
            rz_send[dz] = value
            send(rs_z(dz))

    for copy in sent:
        copy.wait_send()


def coefficients(offsets, tile_of, window, remote, codes, coef, code_s, code_r):
    for i, (dx, dy) in enumerate(offsets):
        sx, sy = tile_of(-dx, -dy)
        at = window(codes, sx, sy)
        remote(at, at, code_s.at[i], code_r.at[i], {"gx": sx, "gy": sy}).wait_recv()

    def lookup(code):
        return sum(TABLE[c] * (code == c).astype(F32) for c in range(4))

    cx, cy = lookup(codes[0]), lookup(codes[1])
    mask = jnp.where(codes[2] == 1, F32(1.0), F32(0.3))
    rows, cols = cx.shape
    row = lax.broadcasted_iota(jnp.int32, cx.shape, 0)
    col = lax.broadcasted_iota(jnp.int32, cx.shape, 1)
    zero = jnp.zeros_like(cx)
    east = jnp.where(row < rows - 1, 0.5 * (cx + pltpu.roll(cx, rows - 1, 0)), zero)
    west = jnp.where(row > 0, 0.5 * (cx + pltpu.roll(cx, 1, 0)), zero)
    north = jnp.where(col < cols - 1, 0.5 * (cy + pltpu.roll(cy, cols - 1, 1)), zero)
    south = jnp.where(col > 0, 0.5 * (cy + pltpu.roll(cy, 1, 1)), zero)
    coef[0] = mask * (1.0 - (east + west + north + south))
    coef[1] = east * pltpu.roll(mask, rows - 1, 0)
    coef[2] = west * pltpu.roll(mask, 1, 0)
    coef[3] = north * pltpu.roll(mask, cols - 1, 1)
    coef[4] = south * pltpu.roll(mask, 1, 1)
    coef[5] = mask * east
    coef[6] = mask * west
    coef[7] = mask * north
    coef[8] = mask * south


def solution(mesh):
    gx_n, gy_n = mesh.shape["gx"], mesh.shape["gy"]
    offsets = [(dx, dy) for dx in (2, 1, 3, 0) for dy in range(1, gy_n)]
    offsets += [(dx, 0) for dx in (2, 1, 3)]
    others = len(offsets)

    def per_device(gradient, perturbation, classes, land_sea):
        tile = gradient.shape[1:]
        grid = (tile[0] * gx_n, tile[1] * gy_n)
        three = (3,) + tile
        dma = pltpu.SemaphoreType.DMA
        any_space = pl.BlockSpec(memory_space=pl.ANY)
        return pl.pallas_call(
            functools.partial(kernel, gx_n, gy_n, offsets),
            out_shape=jax.ShapeDtypeStruct(three, F32),
            in_specs=[any_space] * 4,
            out_specs=pl.BlockSpec(memory_space=pltpu.VMEM),
            scratch_shapes=[
                pltpu.VMEM((BLOCKS,) + three, F32),
                pltpu.VMEM((BLOCKS,) + three, jnp.bfloat16),
                pltpu.VMEM((BLOCKS,) + three, jnp.bfloat16),
                pltpu.VMEM((BLOCKS,) + three, F32),
                pltpu.VMEM((BLOCKS,) + three, F32),
                pltpu.VMEM((3,) + grid, jnp.int32),
                pltpu.VMEM((9,) + grid, F32),
                pltpu.VMEM((LEVELS + 2,) + tile, F32),
                pltpu.VMEM((LEVELS + 2,) + tile, F32),
                pltpu.VMEM((LEVELS + 2,) + tile, F32),
                pltpu.VMEM((2, 3) + grid, F32),
                pltpu.VMEM((gx_n, 3 * gy_n) + tile, F32),
                pltpu.VMEM((gx_n, 3 * gy_n) + tile, F32),
                pltpu.VMEM((LEVELS + 2,) + tile, F32),
                pltpu.VMEM((LEVELS + 2,) + tile, F32),
                pltpu.VMEM((ZH, 7) + three, F32),
                pltpu.VMEM((ZH, 7) + three, F32),
                pltpu.VMEM((ZH,) + three, F32),
                pltpu.VMEM((ZH,) + three, F32),
                dma((5,)),
                dma((ZH,)), dma((ZH,)),
                dma((ZH, 7)), dma((ZH, 7)),
                dma((others,)), dma((others,)),
                dma, dma, dma, dma,
                dma((2, others)), dma((2, others)),
                dma((2, others)), dma((2, others)),
                dma((others + 1,)), dma((others + 1,)),
                dma((ZH, 7)), dma((ZH, 7)),
                dma((ZH,)), dma((ZH,)),
            ],
            compiler_params=pltpu.CompilerParams(collective_id=0, has_side_effects=True),
        )(
            gradient,
            perturbation.reshape((BLOCKS, 2) + three),
            classes,
            land_sea.reshape((1,) + tile),
        )

    placed = (P("mem", "gx", "gy"), P("mem", None, "gx", "gy"), P(None, "gx", "gy"), P("gx", "gy"))
    return jax.shard_map(
        per_device, mesh=mesh, in_specs=placed, out_specs=P("mem", "gx", "gy"), check_vma=False
    )
```

```python
import functools

import jax
import jax.numpy as jnp
from jax import lax
from jax.experimental import pallas as pl
from jax.experimental.pallas import tpu as pltpu
from jax.sharding import PartitionSpec as P

LEVELS = 32
STEPS = 8
TABLE = (0.03, 0.07, 0.12, 0.18)
MESH = pl.DeviceIdType.MESH

ZH = 4
YN = 8
BLOCKS = ZH * YN
F32 = jnp.float32

GROUPS = ((0, 1), (1, 2))
HOPS = (1, 2, -1, -2, 1, 2, -1)
SOURCES = (-1, -2, 1, 2, -3, -4, 3)


def kernel(
    gx_n, gy_n, offsets,
    grad_hbm, pert_hbm, classes_hbm, sea_hbm, out_ref,
    gall, pown, praw, psend, pother, codes, coef,
    wsend, wrecv, wown, field, back, back_other, s_own, s_other,
    rs_send, rs_recv, rz_send, rz_recv,
    loc, agz_s, agz_r, agy_s, agy_r, code_s, code_r, px_s, px_r, w_s, w_r,
    t_s, t_r, b_s, b_r, fw_s, fw_r, rsy_s, rsy_r, rsz_s, rsz_r,
):
    mem = lax.axis_index("mem")
    gx = lax.axis_index("gx")
    gy = lax.axis_index("gy")
    core = lax.rem(mem, 2)
    y = lax.rem(mem // 2, YN)
    zh = mem // (2 * YN)

    def mem_at(z, yy):
        return {"mem": block(z, yy) * 2 + core}

    partner = {"mem": mem + 1 - 2 * core}

    def z_of(dz):
        return zh + (0, 1, -1, 2)[dz]

    def way(dz):
        return 1 if dz % 2 == 0 else -1

    def block(z, yy):
        return lax.rem(z + ZH, ZH) * YN + lax.rem(yy + YN, YN)

    def tile_of(dx, dy):
        return lax.rem(gx + dx + gx_n, gx_n), lax.rem(gy + dy + gy_n, gy_n)

    sent = []

    def remote(src, dst, ssem, rsem, where):
        return pltpu.make_async_remote_copy(
            src_ref=src, dst_ref=dst, send_sem=ssem, recv_sem=rsem,
            device_id=where, device_id_type=MESH,
        )

    def send(copy):
        copy.start()
        sent.append(copy)

    def window(ref, tx, ty):
        return ref.at[
            :, pl.ds(pl.multiple_of(tx * 16, 16), 16), pl.ds(pl.multiple_of(ty * 128, 128), 128)
        ]

    barrier = pltpu.get_barrier_semaphore()
    tiles = [tile_of(dx, dy) for dx, dy in offsets]
    near = [mem_at(z_of(dz), y) for dz in (3, 1, 2)] + [mem_at(zh, y + d) for d in (2, -2, 1, -1)]
    near.append(partner)
    for where in near:
        pl.semaphore_signal(barrier, inc=1, device_id=where, device_id_type=MESH)
    for tx, ty in tiles:
        pl.semaphore_signal(barrier, inc=1, device_id={"gx": tx, "gy": ty}, device_id_type=MESH)
    mine = block(zh, y)
    c_grad = pltpu.make_async_copy(grad_hbm, gall.at[mine], loc.at[0])
    c_cls = pltpu.make_async_copy(classes_hbm, window(codes, gx, gy).at[pl.ds(0, 2)], loc.at[1])
    c_sea = pltpu.make_async_copy(sea_hbm, window(codes, gx, gy).at[pl.ds(2, 1)], loc.at[2])
    c_raw = pltpu.make_async_copy(pert_hbm.at[:, 1 - core], praw, loc.at[3])
    c_own = pltpu.make_async_copy(pert_hbm.at[:, core], pown, loc.at[4])
    for copy in (c_grad, c_cls, c_sea, c_raw, c_own):
        copy.start()
    c_grad.wait()
    pl.semaphore_wait(barrier, len(near) + len(offsets))

    def ag_z(dz):
        at = gall.at[mine]
        return remote(at, at, agz_s.at[dz], agz_r.at[dz], mem_at(z_of(dz), y))

    def ag_z_in(dz):
        k = (0, 2, 1, 3)[dz]
        at = gall.at[block(z_of(dz), y)]
        return remote(at, at, agz_s.at[k], agz_r.at[k], mem_at(z_of(dz), y))

    def ag_y(dz, m):
        hop = HOPS[m] * way(dz)
        at = gall.at[block(z_of(dz), y + SOURCES[m] * way(dz) + hop)]
        return remote(at, at, agy_s.at[dz, m], agy_r.at[dz, m], mem_at(zh, y + hop))

    def ag_y_in(dz, m):
        hop = HOPS[m] * way(dz)
        at = gall.at[block(z_of(dz), y + SOURCES[m] * way(dz))]
        return remote(at, at, agy_s.at[dz, m], agy_r.at[dz, m], mem_at(zh, y - hop))

    def ag_first(dz):
        for m in (1, 3, 0, 2):
            send(ag_y(dz, m))

    def ag_second(dz):
        ag_y_in(dz, 1).wait_recv()
        send(ag_y(dz, 5))
        send(ag_y(dz, 4))
        ag_y_in(dz, 3).wait_recv()
        send(ag_y(dz, 6))

    for dz in (3, 1, 2):
        send(ag_z(dz))
    ag_first(0)

    c_cls.wait()
    c_sea.wait()
    for i, (tx, ty) in enumerate(tiles):
        at = window(codes, gx, gy)
        send(remote(at, at, code_s.at[i], code_r.at[i], {"gx": tx, "gy": ty}))
    c_raw.wait()

    @pl.loop(0, BLOCKS)
    def _(b):
        psend[b] = praw[b].astype(F32)

    swap_p = remote(psend, pother, px_s, px_r, partner)
    send(swap_p)
    c_own.wait()

    wown[...] = jnp.zeros_like(wown)
    wsend[...] = jnp.zeros_like(wsend)

    def add_up(dz, p_ref, w_ref):
        @pl.loop(0, YN, unroll=2)
        def _(yy):
            b = block(z_of(dz), yy)
            levels = pl.ds(lax.rem(6 * b + 3 * core, LEVELS), 3)
            w_ref[levels] = w_ref[levels] + p_ref[b].astype(F32) * gall[b]

    def ag_rest(dz):
        for m in (0, 2, 4, 6, 5):
            ag_y_in(dz, m).wait_recv()

    def wrap(w_ref):
        w_ref[pl.ds(0, 2)] = w_ref[pl.ds(0, 2)] + w_ref[pl.ds(LEVELS, 2)]

    ag_second(0)
    for dz in (1, 2, 3):
        ag_z_in(dz).wait_recv()
        ag_first(dz)
    ag_second(1)
    ag_second(2)
    swap_p.wait_recv()
    ag_rest(0)
    add_up(0, pother, wsend)
    add_up(0, pown, wown)
    ag_second(3)
    coefficients(offsets, tile_of, window, remote, codes, coef, code_s, code_r)
    for dz in (1, 2):
        ag_rest(dz)
        add_up(dz, pother, wsend)
        add_up(dz, pown, wown)
    ag_rest(3)
    add_up(3, pother, wsend)
    wrap(wsend)
    swap_w = remote(wsend, wrecv, w_s, w_r, partner)
    send(swap_w)
    add_up(3, pown, wown)
    wrap(wown)
    swap_w.wait_recv()
    wown[...] = wown[...] + wrecv[...]

    def first_level(tx, ty):
        return 8 * tx + jnp.minimum(3 * ty, 5)

    def level_out(g, i, tx, ty):
        at, n = GROUPS[g]
        return remote(
            wown.at[pl.ds(first_level(tx, ty) + at, n)],
            window(field.at[0], gx, gy).at[pl.ds(at, n)],
            t_s.at[g, i], t_r.at[g, i], {"gx": tx, "gy": ty},
        )

    def level_back(g, i, tx, ty):
        at, n = GROUPS[g]
        return remote(
            window(field.at[0], tx, ty).at[pl.ds(at, n)],
            back.at[gx, pl.ds(3 * gy + at, n)],
            b_s.at[g, i], b_r.at[g, i], {"gx": tx, "gy": ty},
        )

    def forward(i, tx, ty):
        at = pl.ds(3 * ty, 3)
        return remote(back.at[tx, at], back_other.at[tx, at], fw_s.at[i], fw_r.at[i], partner)

    c_field = pltpu.make_async_copy(
        wown.at[pl.ds(first_level(gx, gy), 3)], window(field.at[0], gx, gy), loc.at[0]
    )
    c_field.start()
    for g in range(len(GROUPS)):
        for i, (tx, ty) in enumerate(tiles):
            send(level_out(g, i, tx, ty))
    c_field.wait()
    sources = [tile_of(-dx, -dy) for dx, dy in offsets]

    def step(v, base):
        rows, cols = v.shape
        return (
            coef[0] * v
            + coef[base] * pltpu.roll(v, rows - 1, 0)
            + coef[base + 1] * pltpu.roll(v, 1, 0)
            + coef[base + 2] * pltpu.roll(v, cols - 1, 1)
            + coef[base + 3] * pltpu.roll(v, 1, 1)
        )

    for g in range(len(GROUPS)):
        for i in range(len(offsets)):
            level_out(g, i, gx, gy).wait_recv()
        at, n = GROUPS[g]
        for base in (1, 5):
            @pl.loop(0, STEPS // 2)
            def _(_):
                for lev in range(at, at + n):
                    field[1, lev] = step(field[0, lev], base)
                for lev in range(at, at + n):
                    field[0, lev] = step(field[1, lev], base)
        for i, (tx, ty) in enumerate(tiles):
            send(level_back(g, i, tx, ty))
    c_back = pltpu.make_async_copy(
        window(field.at[0], gx, gy), back.at[gx, pl.ds(3 * gy, 3)], loc.at[0],
    )
    c_back.start()
    c_back.wait()
    send(forward(len(offsets), gx, gy))
    last = len(GROUPS) - 1
    for g in range(len(GROUPS)):
        for i, (sx, sy) in enumerate(sources):
            level_back(g, i, sx, sy).wait_recv()
            if g == last:
                send(forward(i, sx, sy))

    def gathered(ref, s_ref):
        levels = jnp.concatenate([ref[:, 0:6], ref[:, 7:9]], axis=1) * F32(1.0 / 63.0)
        levels = levels.reshape((LEVELS,) + levels.shape[2:])
        s_ref[pl.ds(0, LEVELS)] = levels
        s_ref[pl.ds(LEVELS, 2)] = levels[0:2]

    gathered(back, s_own)
    for i, (sx, sy) in enumerate(sources + [(gx, gy)]):
        forward(i, sx, sy).wait_recv()
    gathered(back_other, s_other)

    def term(dz, yy):
        b = block(z_of(dz), yy)
        levels = pl.ds(lax.rem(6 * b + 3 * core, LEVELS), 3)
        return pown[b].astype(F32) * s_own[levels] + pother[b] * s_other[levels]

    def rs_y(dz, m):
        return remote(
            rs_send.at[dz, m], rs_recv.at[dz, m], rsy_s.at[dz, m], rsy_r.at[dz, m],
            mem_at(zh, y + HOPS[m] * way(dz)),
        )

    def rs_put(dz, m, distance, parts=()):
        value = term(dz, y + distance * way(dz))
        for part in parts:
            rs_y(dz, part).wait_recv()
            value = value + rs_recv[dz, part]
        rs_send[dz, m] = value
        send(rs_y(dz, m))

    def rs_z(dz):
        return remote(
            rz_send.at[dz], rz_recv.at[dz], rsz_s.at[dz], rsz_r.at[dz], mem_at(z_of(dz), y)
        )

    order = (3, 1, 2, 0)
    for dz in order:
        rs_put(dz, 5, 4)
        rs_put(dz, 4, 3)
        rs_put(dz, 6, -3)
    for dz in order:
        rs_put(dz, 0, 1)
        rs_put(dz, 2, -1)
        rs_put(dz, 1, 2, (4, 5))
        rs_put(dz, 3, -2, (6,))
    for dz in order:
        value = term(dz, y)
        for m in (0, 2, 1, 3):
            rs_y(dz, m).wait_recv()
            value = value + rs_recv[dz, m]
        if dz == 0:
            for k in (1, 2, 3):
                rs_z(k).wait_recv()
                value = value + rz_recv[k]
            out_ref[...] = value
        else:
            rz_send[dz] = value
            send(rs_z(dz))

    for copy in sent:
        copy.wait_send()


def coefficients(offsets, tile_of, window, remote, codes, coef, code_s, code_r):
    for i, (dx, dy) in enumerate(offsets):
        sx, sy = tile_of(-dx, -dy)
        at = window(codes, sx, sy)
        remote(at, at, code_s.at[i], code_r.at[i], {"gx": sx, "gy": sy}).wait_recv()

    def lookup(code):
        return sum(TABLE[c] * (code == c).astype(F32) for c in range(4))

    cx, cy = lookup(codes[0]), lookup(codes[1])
    mask = jnp.where(codes[2] == 1, F32(1.0), F32(0.3))
    rows, cols = cx.shape
    row = lax.broadcasted_iota(jnp.int32, cx.shape, 0)
    col = lax.broadcasted_iota(jnp.int32, cx.shape, 1)
    zero = jnp.zeros_like(cx)
    east = jnp.where(row < rows - 1, 0.5 * (cx + pltpu.roll(cx, rows - 1, 0)), zero)
    west = jnp.where(row > 0, 0.5 * (cx + pltpu.roll(cx, 1, 0)), zero)
    north = jnp.where(col < cols - 1, 0.5 * (cy + pltpu.roll(cy, cols - 1, 1)), zero)
    south = jnp.where(col > 0, 0.5 * (cy + pltpu.roll(cy, 1, 1)), zero)
    coef[0] = mask * (1.0 - (east + west + north + south))
    coef[1] = east * pltpu.roll(mask, rows - 1, 0)
    coef[2] = west * pltpu.roll(mask, 1, 0)
    coef[3] = north * pltpu.roll(mask, cols - 1, 1)
    coef[4] = south * pltpu.roll(mask, 1, 1)
    coef[5] = mask * east
    coef[6] = mask * west
    coef[7] = mask * north
    coef[8] = mask * south


def hand_on(source, target):
    target[...] = source[...]


def solution(mesh):
    gx_n, gy_n = mesh.shape["gx"], mesh.shape["gy"]
    offsets = [(dx, dy) for dx in (2, 1, 3, 0) for dy in range(1, gy_n)]
    offsets += [(dx, 0) for dx in (2, 1, 3)]
    others = len(offsets)

    def per_device(gradient, perturbation, classes, land_sea):
        tile = gradient.shape[1:]
        grid = (tile[0] * gx_n, tile[1] * gy_n)
        three = (3,) + tile
        dma = pltpu.SemaphoreType.DMA
        any_space = pl.BlockSpec(memory_space=pl.ANY)
        increment = pl.pallas_call(
            functools.partial(kernel, gx_n, gy_n, offsets),
            out_shape=jax.ShapeDtypeStruct(three, F32),
            in_specs=[any_space] * 4,
            out_specs=pl.BlockSpec(memory_space=pltpu.VMEM),
            scratch_shapes=[
                pltpu.VMEM((BLOCKS,) + three, F32),
                pltpu.VMEM((BLOCKS,) + three, jnp.bfloat16),
                pltpu.VMEM((BLOCKS,) + three, jnp.bfloat16),
                pltpu.VMEM((BLOCKS,) + three, F32),
                pltpu.VMEM((BLOCKS,) + three, F32),
                pltpu.VMEM((3,) + grid, jnp.int32),
                pltpu.VMEM((9,) + grid, F32),
                pltpu.VMEM((LEVELS + 2,) + tile, F32),
                pltpu.VMEM((LEVELS + 2,) + tile, F32),
                pltpu.VMEM((LEVELS + 2,) + tile, F32),
                pltpu.VMEM((2, 3) + grid, F32),
                pltpu.VMEM((gx_n, 3 * gy_n) + tile, F32),
                pltpu.VMEM((gx_n, 3 * gy_n) + tile, F32),
                pltpu.VMEM((LEVELS + 2,) + tile, F32),
                pltpu.VMEM((LEVELS + 2,) + tile, F32),
                pltpu.VMEM((ZH, 7) + three, F32),
                pltpu.VMEM((ZH, 7) + three, F32),
                pltpu.VMEM((ZH,) + three, F32),
                pltpu.VMEM((ZH,) + three, F32),
                dma((5,)),
                dma((ZH,)), dma((ZH,)),
                dma((ZH, 7)), dma((ZH, 7)),
                dma((others,)), dma((others,)),
                dma, dma, dma, dma,
                dma((2, others)), dma((2, others)),
                dma((2, others)), dma((2, others)),
                dma((others + 1,)), dma((others + 1,)),
                dma((ZH, 7)), dma((ZH, 7)),
                dma((ZH,)), dma((ZH,)),
            ],
            compiler_params=pltpu.CompilerParams(collective_id=0, has_side_effects=True),
        )(
            gradient,
            perturbation.reshape((BLOCKS, 2) + three),
            classes,
            land_sea.reshape((1,) + tile),
        )
        return pl.pallas_call(hand_on, out_shape=jax.ShapeDtypeStruct(three, F32))(increment)

    placed = (P("mem", "gx", "gy"), P("mem", None, "gx", "gy"), P(None, "gx", "gy"), P("gx", "gy"))
    return jax.shard_map(
        per_device, mesh=mesh, in_specs=placed, out_specs=P("mem", "gx", "gy"), check_vma=False
    )
```

```python
import functools

import jax
import jax.numpy as jnp
from jax import lax
from jax.experimental import pallas as pl
from jax.experimental.pallas import tpu as pltpu
from jax.sharding import PartitionSpec as P

LEVELS = 32
STEPS = 8
TABLE = (0.03, 0.07, 0.12, 0.18)
MESH = pl.DeviceIdType.MESH

ZH = 4
YN = 8
BLOCKS = ZH * YN
F32 = jnp.float32

GROUPS = ((0, 1), (1, 2))
HOPS = (1, 2, -1, -2, 1, 2, -1)
SOURCES = (-1, -2, 1, 2, -3, -4, 3)


def kernel(
    gx_n, gy_n, offsets,
    grad_hbm, pert_hbm, classes_hbm, sea_hbm, out_ref,
    gall, pown, praw, psend, pother, codes, coef,
    wsend, wrecv, wown, field, back, back_other, s_own, s_other,
    rs_send, rs_recv, rz_send, rz_recv,
    loc, agz_s, agz_r, agy_s, agy_r, code_s, code_r, px_s, px_r, w_s, w_r,
    t_s, t_r, b_s, b_r, fw_s, fw_r, rsy_s, rsy_r, rsz_s, rsz_r,
):
    mem = lax.axis_index("mem")
    gx = lax.axis_index("gx")
    gy = lax.axis_index("gy")
    core = lax.rem(mem, 2)
    y = lax.rem(mem // 2, YN)
    zh = mem // (2 * YN)

    def mem_at(z, yy):
        return {"mem": block(z, yy) * 2 + core}

    partner = {"mem": mem + 1 - 2 * core}

    def z_of(dz):
        return zh + (0, 1, -1, 2)[dz]

    def way(dz):
        return 1 if dz % 2 == 0 else -1

    def block(z, yy):
        return lax.rem(z + ZH, ZH) * YN + lax.rem(yy + YN, YN)

    def tile_of(dx, dy):
        return lax.rem(gx + dx + gx_n, gx_n), lax.rem(gy + dy + gy_n, gy_n)

    sent = []

    def remote(src, dst, ssem, rsem, where):
        return pltpu.make_async_remote_copy(
            src_ref=src, dst_ref=dst, send_sem=ssem, recv_sem=rsem,
            device_id=where, device_id_type=MESH,
        )

    def send(copy):
        copy.start()
        sent.append(copy)

    def window(ref, tx, ty):
        return ref.at[
            :, pl.ds(pl.multiple_of(tx * 16, 16), 16), pl.ds(pl.multiple_of(ty * 128, 128), 128)
        ]

    barrier = pltpu.get_barrier_semaphore()
    tiles = [tile_of(dx, dy) for dx, dy in offsets]
    near = [mem_at(z_of(dz), y) for dz in (3, 1, 2)] + [mem_at(zh, y + d) for d in (2, -2, 1, -1)]
    near.append(partner)
    for where in near:
        pl.semaphore_signal(barrier, inc=1, device_id=where, device_id_type=MESH)
    for tx, ty in tiles:
        pl.semaphore_signal(barrier, inc=1, device_id={"gx": tx, "gy": ty}, device_id_type=MESH)
    mine = block(zh, y)
    c_grad = pltpu.make_async_copy(grad_hbm, gall.at[mine], loc.at[0])
    c_cls = pltpu.make_async_copy(classes_hbm, window(codes, gx, gy).at[pl.ds(0, 2)], loc.at[1])
    c_sea = pltpu.make_async_copy(sea_hbm, window(codes, gx, gy).at[pl.ds(2, 1)], loc.at[2])
    c_raw = pltpu.make_async_copy(pert_hbm.at[:, 1 - core], praw, loc.at[3])
    c_own = pltpu.make_async_copy(pert_hbm.at[:, core], pown, loc.at[4])
    for copy in (c_grad, c_cls, c_sea, c_raw, c_own):
        copy.start()
    c_grad.wait()
    pl.semaphore_wait(barrier, len(near) + len(offsets))

    def ag_z(dz):
        at = gall.at[mine]
        return remote(at, at, agz_s.at[dz], agz_r.at[dz], mem_at(z_of(dz), y))

    def ag_z_in(dz):
        k = (0, 2, 1, 3)[dz]
        at = gall.at[block(z_of(dz), y)]
        return remote(at, at, agz_s.at[k], agz_r.at[k], mem_at(z_of(dz), y))

    def ag_y(dz, m):
        hop = HOPS[m] * way(dz)
        at = gall.at[block(z_of(dz), y + SOURCES[m] * way(dz) + hop)]
        return remote(at, at, agy_s.at[dz, m], agy_r.at[dz, m], mem_at(zh, y + hop))

    def ag_y_in(dz, m):
        hop = HOPS[m] * way(dz)
        at = gall.at[block(z_of(dz), y + SOURCES[m] * way(dz))]
        return remote(at, at, agy_s.at[dz, m], agy_r.at[dz, m], mem_at(zh, y - hop))

    def ag_first(dz):
        for m in (1, 3, 0, 2):
            send(ag_y(dz, m))

    def ag_second(dz):
        ag_y_in(dz, 1).wait_recv()
        send(ag_y(dz, 5))
        send(ag_y(dz, 4))
        ag_y_in(dz, 3).wait_recv()
        send(ag_y(dz, 6))

    for dz in (3, 1, 2):
        send(ag_z(dz))
    ag_first(0)

    c_cls.wait()
    c_sea.wait()
    for i, (tx, ty) in enumerate(tiles):
        at = window(codes, gx, gy)
        send(remote(at, at, code_s.at[i], code_r.at[i], {"gx": tx, "gy": ty}))
    c_raw.wait()

    @pl.loop(0, BLOCKS)
    def _(b):
        psend[b] = praw[b].astype(F32)

    swap_p = remote(psend, pother, px_s, px_r, partner)
    send(swap_p)
    c_own.wait()

    wown[...] = jnp.zeros_like(wown)
    wsend[...] = jnp.zeros_like(wsend)

    def add_up(dz, p_ref, w_ref):
        @pl.loop(0, YN, unroll=2)
        def _(yy):
            b = block(z_of(dz), yy)
            levels = pl.ds(lax.rem(6 * b + 3 * core, LEVELS), 3)
            w_ref[levels] = w_ref[levels] + p_ref[b].astype(F32) * gall[b]

    def ag_rest(dz):
        for m in (0, 2, 4, 6, 5):
            ag_y_in(dz, m).wait_recv()

    def wrap(w_ref):
        w_ref[pl.ds(0, 2)] = w_ref[pl.ds(0, 2)] + w_ref[pl.ds(LEVELS, 2)]

    ag_second(0)
    for dz in (1, 2, 3):
        ag_z_in(dz).wait_recv()
        ag_first(dz)
    ag_second(1)
    ag_second(2)
    swap_p.wait_recv()
    ag_rest(0)
    add_up(0, pother, wsend)
    add_up(0, pown, wown)
    ag_second(3)
    coefficients(offsets, tile_of, window, remote, codes, coef, code_s, code_r)
    for dz in (1, 2):
        ag_rest(dz)
        add_up(dz, pother, wsend)
        add_up(dz, pown, wown)
    ag_rest(3)
    add_up(3, pother, wsend)
    wrap(wsend)
    swap_w = remote(wsend, wrecv, w_s, w_r, partner)
    send(swap_w)
    add_up(3, pown, wown)
    wrap(wown)
    swap_w.wait_recv()
    wown[...] = wown[...] + wrecv[...]

    def first_level(tx, ty):
        return 8 * tx + jnp.minimum(3 * ty, 5)

    def level_out(g, i, tx, ty):
        at, n = GROUPS[g]
        return remote(
            wown.at[pl.ds(first_level(tx, ty) + at, n)],
            window(field.at[0], gx, gy).at[pl.ds(at, n)],
            t_s.at[g, i], t_r.at[g, i], {"gx": tx, "gy": ty},
        )

    def level_back(g, i, tx, ty):
        at, n = GROUPS[g]
        return remote(
            window(field.at[0], tx, ty).at[pl.ds(at, n)],
            back.at[gx, pl.ds(3 * gy + at, n)],
            b_s.at[g, i], b_r.at[g, i], {"gx": tx, "gy": ty},
        )

    def forward(i, tx, ty):
        at = pl.ds(3 * ty, 3)
        return remote(back.at[tx, at], back_other.at[tx, at], fw_s.at[i], fw_r.at[i], partner)

    c_field = pltpu.make_async_copy(
        wown.at[pl.ds(first_level(gx, gy), 3)], window(field.at[0], gx, gy), loc.at[0]
    )
    c_field.start()
    for g in range(len(GROUPS)):
        for i, (tx, ty) in enumerate(tiles):
            send(level_out(g, i, tx, ty))
    c_field.wait()
    sources = [tile_of(-dx, -dy) for dx, dy in offsets]

    def step(v, base):
        rows, cols = v.shape
        return (
            coef[0] * v
            + coef[base] * pltpu.roll(v, rows - 1, 0)
            + coef[base + 1] * pltpu.roll(v, 1, 0)
            + coef[base + 2] * pltpu.roll(v, cols - 1, 1)
            + coef[base + 3] * pltpu.roll(v, 1, 1)
        )

    for g in range(len(GROUPS)):
        for i in range(len(offsets)):
            level_out(g, i, gx, gy).wait_recv()
        at, n = GROUPS[g]
        for base in (1, 5):
            @pl.loop(0, STEPS // 2)
            def _(_):
                for lev in range(at, at + n):
                    field[1, lev] = step(field[0, lev], base)
                for lev in range(at, at + n):
                    field[0, lev] = step(field[1, lev], base)
        for i, (tx, ty) in enumerate(tiles):
            send(level_back(g, i, tx, ty))
    c_back = pltpu.make_async_copy(
        window(field.at[0], gx, gy), back.at[gx, pl.ds(3 * gy, 3)], loc.at[0],
    )
    c_back.start()
    c_back.wait()
    send(forward(len(offsets), gx, gy))
    last = len(GROUPS) - 1
    for g in range(len(GROUPS)):
        for i, (sx, sy) in enumerate(sources):
            level_back(g, i, sx, sy).wait_recv()
            if g == last:
                send(forward(i, sx, sy))

    def gathered(ref, s_ref):
        levels = jnp.concatenate([ref[:, 0:6], ref[:, 7:9]], axis=1) * F32(1.0 / 63.0)
        levels = levels.reshape((LEVELS,) + levels.shape[2:])
        s_ref[pl.ds(0, LEVELS)] = levels
        s_ref[pl.ds(LEVELS, 2)] = levels[0:2]

    gathered(back, s_own)
    for i, (sx, sy) in enumerate(sources + [(gx, gy)]):
        forward(i, sx, sy).wait_recv()
    gathered(back_other, s_other)

    def term(dz, yy):
        b = block(z_of(dz), yy)
        levels = pl.ds(lax.rem(6 * b + 3 * core, LEVELS), 3)
        return pown[b].astype(F32) * s_own[levels] + pother[b] * s_other[levels]

    def rs_y(dz, m):
        return remote(
            rs_send.at[dz, m], rs_recv.at[dz, m], rsy_s.at[dz, m], rsy_r.at[dz, m],
            mem_at(zh, y + HOPS[m] * way(dz)),
        )

    def rs_put(dz, m, distance, parts=()):
        value = term(dz, y + distance * way(dz))
        for part in parts:
            rs_y(dz, part).wait_recv()
            value = value + rs_recv[dz, part]
        rs_send[dz, m] = value
        send(rs_y(dz, m))

    def rs_z(dz):
        return remote(
            rz_send.at[dz], rz_recv.at[dz], rsz_s.at[dz], rsz_r.at[dz], mem_at(z_of(dz), y)
        )

    order = (3, 1, 2, 0)
    for dz in order:
        rs_put(dz, 5, 4)
        rs_put(dz, 4, 3)
        rs_put(dz, 6, -3)
    for dz in order:
        rs_put(dz, 0, 1)
        rs_put(dz, 2, -1)
        rs_put(dz, 3, -2, (6,))
        rs_put(dz, 1, 2, (4, 5))
    for dz in order:
        value = term(dz, y)
        for m in (0, 2, 1, 3):
            rs_y(dz, m).wait_recv()
            value = value + rs_recv[dz, m]
        if dz == 0:
            for k in (1, 2, 3):
                rs_z(k).wait_recv()
                value = value + rz_recv[k]
            out_ref[...] = value
        else:
            rz_send[dz] = value
            send(rs_z(dz))

    for copy in sent:
        copy.wait_send()


def coefficients(offsets, tile_of, window, remote, codes, coef, code_s, code_r):
    for i, (dx, dy) in enumerate(offsets):
        sx, sy = tile_of(-dx, -dy)
        at = window(codes, sx, sy)
        remote(at, at, code_s.at[i], code_r.at[i], {"gx": sx, "gy": sy}).wait_recv()

    def lookup(code):
        return sum(TABLE[c] * (code == c).astype(F32) for c in range(4))

    cx, cy = lookup(codes[0]), lookup(codes[1])
    mask = jnp.where(codes[2] == 1, F32(1.0), F32(0.3))
    rows, cols = cx.shape
    row = lax.broadcasted_iota(jnp.int32, cx.shape, 0)
    col = lax.broadcasted_iota(jnp.int32, cx.shape, 1)
    zero = jnp.zeros_like(cx)
    east = jnp.where(row < rows - 1, 0.5 * (cx + pltpu.roll(cx, rows - 1, 0)), zero)
    west = jnp.where(row > 0, 0.5 * (cx + pltpu.roll(cx, 1, 0)), zero)
    north = jnp.where(col < cols - 1, 0.5 * (cy + pltpu.roll(cy, cols - 1, 1)), zero)
    south = jnp.where(col > 0, 0.5 * (cy + pltpu.roll(cy, 1, 1)), zero)
    coef[0] = mask * (1.0 - (east + west + north + south))
    coef[1] = east * pltpu.roll(mask, rows - 1, 0)
    coef[2] = west * pltpu.roll(mask, 1, 0)
    coef[3] = north * pltpu.roll(mask, cols - 1, 1)
    coef[4] = south * pltpu.roll(mask, 1, 1)
    coef[5] = mask * east
    coef[6] = mask * west
    coef[7] = mask * north
    coef[8] = mask * south


def hand_on(source, target):
    target[...] = source[...]


def solution(mesh):
    gx_n, gy_n = mesh.shape["gx"], mesh.shape["gy"]
    offsets = [(dx, dy) for dx in (2, 1, 3, 0) for dy in range(1, gy_n)]
    offsets += [(dx, 0) for dx in (2, 1, 3)]
    others = len(offsets)

    def per_device(gradient, perturbation, classes, land_sea):
        tile = gradient.shape[1:]
        grid = (tile[0] * gx_n, tile[1] * gy_n)
        three = (3,) + tile
        dma = pltpu.SemaphoreType.DMA
        any_space = pl.BlockSpec(memory_space=pl.ANY)
        increment = pl.pallas_call(
            functools.partial(kernel, gx_n, gy_n, offsets),
            out_shape=jax.ShapeDtypeStruct(three, F32),
            in_specs=[any_space] * 4,
            out_specs=pl.BlockSpec(memory_space=pltpu.VMEM),
            scratch_shapes=[
                pltpu.VMEM((BLOCKS,) + three, F32),
                pltpu.VMEM((BLOCKS,) + three, jnp.bfloat16),
                pltpu.VMEM((BLOCKS,) + three, jnp.bfloat16),
                pltpu.VMEM((BLOCKS,) + three, F32),
                pltpu.VMEM((BLOCKS,) + three, F32),
                pltpu.VMEM((3,) + grid, jnp.int32),
                pltpu.VMEM((9,) + grid, F32),
                pltpu.VMEM((LEVELS + 2,) + tile, F32),
                pltpu.VMEM((LEVELS + 2,) + tile, F32),
                pltpu.VMEM((LEVELS + 2,) + tile, F32),
                pltpu.VMEM((2, 3) + grid, F32),
                pltpu.VMEM((gx_n, 3 * gy_n) + tile, F32),
                pltpu.VMEM((gx_n, 3 * gy_n) + tile, F32),
                pltpu.VMEM((LEVELS + 2,) + tile, F32),
                pltpu.VMEM((LEVELS + 2,) + tile, F32),
                pltpu.VMEM((ZH, 7) + three, F32),
                pltpu.VMEM((ZH, 7) + three, F32),
                pltpu.VMEM((ZH,) + three, F32),
                pltpu.VMEM((ZH,) + three, F32),
                dma((5,)),
                dma((ZH,)), dma((ZH,)),
                dma((ZH, 7)), dma((ZH, 7)),
                dma((others,)), dma((others,)),
                dma, dma, dma, dma,
                dma((2, others)), dma((2, others)),
                dma((2, others)), dma((2, others)),
                dma((others + 1,)), dma((others + 1,)),
                dma((ZH, 7)), dma((ZH, 7)),
                dma((ZH,)), dma((ZH,)),
            ],
            compiler_params=pltpu.CompilerParams(collective_id=0, has_side_effects=True),
        )(
            gradient,
            perturbation.reshape((BLOCKS, 2) + three),
            classes,
            land_sea.reshape((1,) + tile),
        )
        return pl.pallas_call(hand_on, out_shape=jax.ShapeDtypeStruct(three, F32))(increment)

    placed = (P("mem", "gx", "gy"), P("mem", None, "gx", "gy"), P(None, "gx", "gy"), P("gx", "gy"))
    return jax.shard_map(
        per_device, mesh=mesh, in_specs=placed, out_specs=P("mem", "gx", "gy"), check_vma=False
    )
```
